128 devices in a mesh: tok: 4 (over y), seq: 16 (over z, x), kv: 2 (over core).
Axes of the slice: x: 4, y: 4, z: 4, core: 2. Of those that a mesh axis runs over, the one named last changes fastest.
Arguments:
- token_ids: int32 [64, 4], replicated, may hold values from 0 to 32767
- request_order: int32 [64], replicated, may hold values from 0 to 63, each once
- cache_lengths: int32 [64], replicated, may hold values from 1 to 16384, 524288 in all
- embed_table: bfloat16 [32768, 2048], P(('tok', 'kv'), 'seq'), may hold values from -3 to 3
- attn_gain: bfloat16 [2048], replicated, may hold values from 0.099609375 to 1.8984375
- proj_query: bfloat16 [2048, 2048], P(None, ('tok', 'kv')), may hold values from -0.125 to 0.125
- proj_kv: bfloat16 [2048, 8, 128], P(None, ('tok', 'kv')), may hold values from -0.125 to 0.125
- kv_cache: bfloat16 [64, 16384, 8, 128], P(None, 'seq', ('tok', 'kv')), may hold values from -125 to 125, as said below
- proj_out: bfloat16 [2048, 2048], P(('tok', 'kv'), 'seq'), may hold values from -0.25 to 0.25
- mlp_gain: bfloat16 [2048], replicated, may hold values from 0.099609375 to 1.8984375
- proj_gate: bfloat16 [2048, 8192], P(None, 'seq'), may hold values from -0.125 to 0.125
- proj_up: bfloat16 [2048, 8192], P(None, 'seq'), may hold values from -0.125 to 0.125
- proj_down: bfloat16 [8192, 2048], P('seq'), may hold values from -0.0625 to 0.0625
Outputs:
- hidden_out: bfloat16 [64, 4, 2048], P(('tok', 'kv'), None, 'seq')
The draws below stay inside these ranges and needn't reach their ends.
Inputs may be any that keep to these rules, and one draw needn't show every extreme that they name: `request_order`: every request stands in exactly one slot. `cache_lengths`: the lengths sum to 524288 and the largest equals 16384. `kv_cache`: cached keys are already rotated to their positions.
All inputs are finite; a program needn't handle non-finite values.
Results may differ from the reference program's by a relative error of at most 0.018.
The reference program's roundings to bfloat16 on the way count: a program that leaves them out, or rounds other values in their place, can miss the bound.
Values may be sent and summed in bfloat16 or wider, within the bound.
A program may use at most 128 MiB of HBM per device.

```python
import math
import jax
import jax.numpy as jnp
import numpy as np
from jax import lax

D = 2048
H = 32
HD = 64
KVH = 8
FF = 8192
VOCAB = 32768
STEPS = 4
REQ = 64
CTX_DEV = 1024
CTX = 16384
N_SEQ = 16


def draw_kv_cache(key, part):

    def draw_request(request_index):
        request_key = jax.random.fold_in(jax.random.fold_in(key, 7001), request_index)
        keys_seed, vals_seed = jax.random.split(request_key, 2)
        grid_shape = (CTX, KVH, HD)
        key_part = jax.random.truncated_normal(keys_seed, -4.0, 4.0, grid_shape) * 1.5
        value_part = jax.random.truncated_normal(vals_seed, -4.0, 4.0, grid_shape)
        return jnp.concatenate([key_part, value_part], axis=-1)
    return lax.map(draw_request, jnp.arange(REQ, dtype=jnp.int32)).astype(jnp.bfloat16)


def touch_ends(values, rng, low, top_value):
    longest = values.shape.index(max(values.shape))
    spots = []
    for shift in (0, 1):
        where = [jax.random.randint(jax.random.fold_in(rng, axis), (), 0, length) for axis, length in enumerate(values.shape)]
        where[longest] = (where[longest] + shift) % values.shape[longest]
        spots.append(tuple(where))
    return values.at[spots[0]].set(low).at[spots[1]].set(top_value)


def shard_levels(stream_key, dims, pieces, least, high):
    gain, own = 1.0, jax.random.fold_in(stream_key, 6)
    for dim, shards_of in pieces:
        draws = jnp.exp(jax.random.uniform(jax.random.fold_in(own, dim), (shards_of,), jnp.float32, least / len(pieces), high / len(pieces)))
        gain = gain * jnp.repeat(draws, dims[dim] // shards_of).reshape([-1 if axis == dim else 1 for axis in range(len(dims))])
    return gain


def cumulative_ranks(count, slope):
    loads = [(1 << 20) // math.isqrt(standing ** slope) + 1 for standing in range(1, count + 1)]
    scale = 1 + sum(loads) // (1 << 30)
    return np.cumsum(np.array([max(1, weight // scale) for weight in loads]))


def skewed_ids(stream_key, extent, number_of, slope):
    listing = cumulative_ranks(number_of, slope)
    ticket = jax.random.randint(jax.random.fold_in(stream_key, 1), extent, 0, int(listing[number_of - 1]))
    standing = jnp.searchsorted(jnp.asarray(listing, jnp.int32), ticket, side="right")
    return jax.random.permutation(jax.random.fold_in(stream_key, 2), number_of)[standing].astype(jnp.int32)


def length_profile(amount, total, limit, skew):
    loads = [(1 << 20) // math.isqrt(grade ** skew) + 1 for grade in range(2, amount + 1)]
    surplus, holding = total - limit - (amount - 1), [1] * (amount - 1)
    while surplus > 0:
        free = [i for i in range(amount - 1) if holding[i] < limit]
        whole, budget = sum([loads[i] for i in free]), surplus
        for i in free:
            more = min(limit - holding[i], max(1, budget * loads[i] // whole), surplus)
            holding[i] = holding[i] + more
            surplus = surplus - more
    return np.array([limit] + holding)


def ragged(own_key, count, total, limit, skew):
    if count == 2:
        one = jax.random.randint(own_key, (), max(1, total - limit), min(limit, total - 1) + 1)
        return jnp.stack([one, total - one])
    tallies = jnp.asarray(length_profile(count, total, limit, skew), jnp.int32)
    couples = (count - 1) // 2
    donor, taker = tallies[1:1 + 2 * couples:2], tallies[2:2 + 2 * couples:2]
    room = jnp.minimum(donor - 1, limit - taker)
    passed = jax.random.randint(jax.random.fold_in(own_key, 1), (couples,), 0, 1 << 20) % (room + 1)
    tallies = tallies.at[1:1 + 2 * couples:2].set(donor - passed).at[2:2 + 2 * couples:2].set(taker + passed)
    return tallies[jax.random.permutation(jax.random.fold_in(own_key, 2), count)]


def bell_draw(key, extent, scale, reach, pieces=(), kind=jnp.bfloat16):
    gain = shard_levels(key, extent, pieces, -0.22, 0.18) if pieces else 1.0
    array = jax.random.normal(key, extent, jnp.float32) * scale * gain
    return jnp.minimum(jnp.maximum(array, -reach), reach).astype(kind)


def setup_inputs(seed: int = 0) -> dict:
    splits = jax.random.split(jax.random.key(seed), 14)
    return {
        "token_ids": touch_ends(skewed_ids(splits[0], (REQ, STEPS), VOCAB, 2), jax.random.fold_in(splits[0], 3), 0, VOCAB - 1).astype(jnp.int32),
        "request_order": jax.random.permutation(splits[1], REQ).astype(jnp.int32),
        "cache_lengths": ragged(splits[2], REQ, REQ * CTX // 2, CTX, 2).astype(jnp.int32),
        "embed_table": bell_draw(splits[3], (VOCAB, D), 0.5, 3.0, ((0, 8), (1, 16))),
        "attn_gain": jnp.clip(1.0 + 0.18 * jax.random.normal(splits[4], (D,), jnp.float32), 0.099609375, 1.8984375).astype(jnp.bfloat16),
        "proj_query": bell_draw(splits[5], (D, H * HD), D ** -0.5, 0.125, ((1, 8),)),
        "proj_kv": bell_draw(splits[6], (D, KVH, 2 * HD), D ** -0.5, 0.125, ((1, 8),)),
        "kv_cache": draw_kv_cache(jax.random.fold_in(splits[13], 71), 0),
        "proj_out": bell_draw(splits[8], (H * HD, D), (H * HD // 4) ** -0.5, 0.25, ((0, 8), (1, 16))),
        "mlp_gain": jnp.clip(1.0 + 0.18 * jax.random.normal(splits[9], (D,), jnp.float32), 0.099609375, 1.8984375).astype(jnp.bfloat16),
        "proj_gate": bell_draw(splits[10], (D, FF), D ** -0.5, 0.125, ((1, 16),)),
        "proj_up": bell_draw(splits[11], (D, FF), D ** -0.5, 0.125, ((1, 16),)),
        "proj_down": bell_draw(splits[12], (FF, D), FF ** -0.5, 0.0625, ((0, 16),)),
    }


EPSILON = 1e-05
ROPE_BASE = 1000000.0
FLOOR_SCORE = -1e+30

def rotate(vector, position):
    half_dim = vector.shape[-1] // 2
    frequency = ROPE_BASE ** (-(jnp.arange(half_dim, dtype=jnp.float32) * 2.0 / vector.shape[-1]))
    angles = position[..., None] * frequency
    cosine = jnp.cos(angles)
    sine_part = jnp.sin(angles)
    front_half = vector[..., :half_dim]
    back_half = vector[..., half_dim:]
    return jnp.concatenate([front_half * cosine - back_half * sine_part, back_half * cosine + front_half * sine_part], axis=-1)

def reference(token_ids, request_order, cache_lengths, embed_table, attn_gain, proj_query, proj_kv, kv_cache, proj_out, mlp_gain, proj_gate, proj_up, proj_down):
    group = H // KVH
    scale = HD ** (-0.5)
    embedded = embed_table[token_ids]
    widened = embedded.astype(jnp.float32)
    inv_attn = lax.rsqrt(lax.optimization_barrier(jnp.mean(widened * widened, axis=-1)) + EPSILON).reshape(REQ * STEPS, 1)
    scaled = (widened * attn_gain.astype(jnp.float32)).astype(jnp.bfloat16).reshape(REQ * STEPS, D)
    q_raw = jnp.dot(scaled, proj_query, preferred_element_type=jnp.float32) * inv_attn
    kv_raw = jnp.dot(scaled, proj_kv.reshape(D, KVH * 2 * HD), preferred_element_type=jnp.float32) * inv_attn
    kv_raw = kv_raw.reshape(REQ, STEPS, KVH, 2 * HD)
    position = (cache_lengths[:, None] + jnp.arange(STEPS, dtype=jnp.int32)[None, :]).astype(jnp.float32)
    query = rotate(q_raw.reshape(REQ, STEPS, H, HD), position[:, :, None]).astype(jnp.bfloat16)
    new_keys = rotate(kv_raw[..., :HD], position[:, :, None]).astype(jnp.bfloat16)
    new_values = kv_raw[..., HD:].astype(jnp.bfloat16)

    def attend(request_item):
        query_row, cache_row, key_row, value_row, length = request_item
        grouped = query_row.reshape(STEPS, KVH, group, HD).astype(jnp.float32)
        key_part = cache_row[..., :HD].astype(jnp.float32).reshape(N_SEQ, CTX_DEV, KVH, HD)
        value_part = cache_row[..., HD:].astype(jnp.float32).reshape(N_SEQ, CTX_DEV, KVH, HD)
        scores = jnp.einsum('jkgd,bpkd->bjkgp', grouped, key_part) * scale
        places = jnp.arange(N_SEQ, dtype=jnp.int32)[:, None] * CTX_DEV + jnp.arange(CTX_DEV, dtype=jnp.int32)[None, :]
        is_live = (places < length)[:, None, None, None, :]
        masked = jnp.where(is_live, scores, FLOOR_SCORE)
        block_peak = lax.optimization_barrier(jnp.max(masked, axis=-1))
        rounded = jnp.where(is_live, jnp.exp(masked - block_peak[..., None]), 0.0).astype(jnp.bfloat16)
        weights = lax.optimization_barrier(rounded).astype(jnp.float32)
        block_mass = lax.optimization_barrier(jnp.sum(weights, axis=-1))
        block_accum = jnp.einsum('bjkgp,bpkd->bjkgd', weights, value_part)
        fresh_scores = jnp.einsum('jkgd,ikd->jkgi', grouped, key_row.astype(jnp.float32)) * scale
        causal = (jnp.arange(STEPS)[:, None] >= jnp.arange(STEPS)[None, :])[:, None, None, :]
        fresh_masked = jnp.where(causal, fresh_scores, FLOOR_SCORE)
        fresh_peak = lax.optimization_barrier(jnp.max(fresh_masked, axis=-1))
        fresh_round = jnp.where(causal, jnp.exp(fresh_masked - fresh_peak[..., None]), 0.0).astype(jnp.bfloat16)
        fresh_weights = lax.optimization_barrier(fresh_round).astype(jnp.float32)
        fresh_mass = lax.optimization_barrier(jnp.sum(fresh_weights, axis=-1))
        fresh_accum = jnp.einsum('jkgi,ikd->jkgd', fresh_weights, value_row.astype(jnp.float32))
        highest = jnp.maximum(lax.optimization_barrier(jnp.max(block_peak, axis=0)), fresh_peak)
        factor = jnp.exp(block_peak - highest[None])
        fresh_factor = jnp.exp(fresh_peak - highest)
        numer = lax.optimization_barrier(jnp.sum(block_accum * factor[..., None], axis=0)) + fresh_accum * fresh_factor[..., None]
        denom = lax.optimization_barrier(jnp.sum(block_mass * factor, axis=0)) + fresh_mass * fresh_factor
        return (numer / denom[..., None]).astype(jnp.bfloat16).reshape(STEPS, H * HD)
    attended = lax.map(attend, (query, kv_cache, new_keys, new_values, cache_lengths))
    attn_part = jnp.dot(attended.reshape(REQ * STEPS, H * HD), proj_out, preferred_element_type=jnp.float32)
    mid = (widened.reshape(REQ * STEPS, D) + attn_part).astype(jnp.bfloat16)
    mid_wide = mid.astype(jnp.float32)
    inv_mlp = lax.rsqrt(lax.optimization_barrier(jnp.mean(mid_wide * mid_wide, axis=-1)) + EPSILON)[:, None]
    scaled_mid = (mid_wide * mlp_gain.astype(jnp.float32)).astype(jnp.bfloat16)
    gate = jnp.dot(scaled_mid, proj_gate, preferred_element_type=jnp.float32) * inv_mlp
    upward = jnp.dot(scaled_mid, proj_up, preferred_element_type=jnp.float32) * inv_mlp
    hidden = (jax.nn.silu(gate) * upward).astype(jnp.bfloat16)
    result = (mid_wide + jnp.dot(hidden, proj_down, preferred_element_type=jnp.float32)).astype(jnp.bfloat16)
    return result.reshape(REQ, STEPS, D)[request_order]
```

```python
import functools

import jax
import jax.numpy as jnp
import numpy as np
from jax import lax
from jax.experimental import pallas as pl
from jax.experimental.pallas import tpu as pltpu
from jax.sharding import PartitionSpec as P

EPSILON = 1e-05
ROPE_BASE = 1000000.0
FLOOR_SCORE = -1e30
MESH = pl.DeviceIdType.MESH
F32 = jnp.float32
BF16 = jnp.bfloat16


def iota(shape, dim):
    return lax.broadcasted_iota(jnp.int32, shape, dim)


def dot_nt(a, b):
    return lax.dot_general(a, b, (((1,), (1,)), ((), ())), preferred_element_type=F32)


def dot(a, b):
    return jnp.dot(a, b, preferred_element_type=F32)


def layer_kernel(
    n_tok,
    n_seq,
    n_kv,
    ids_ref,
    order_ref,
    len_ref,
    gain_ref,
    freq_ref,
    table_hbm,
    wq_hbm,
    wkv_hbm,
    cache_hbm,
    wo_hbm,
    wg_hbm,
    wu_hbm,
    wd_hbm,
    out_ref,
    table,
    wq,
    wkv,
    cache,
    wo,
    wg,
    wu,
    wd,
    ids_v,
    x_send,
    x_recv,
    x_all,
    x_rows,
    q_all,
    q_rows,
    s_scr,
    p_scr,
    acc_send,
    acc_recv,
    st_send,
    st_recv,
    st_t,
    at_all,
    o_send,
    o_recv,
    mid_all,
    d_send,
    d_recv,
    load_sem,
    send_sem,
    yc_sem,
    seq_sem,
):
    n_own = n_tok * n_kv
    tok = lax.axis_index("tok")
    seq = lax.axis_index("seq")
    kv = lax.axis_index("kv")
    own = tok * n_kv + kv
    vocab = table.shape[0]
    ctx = cache.shape[1]
    n_req = cache.shape[0]
    steps = 4
    rows_own = x_all.shape[1]
    rows_seq = x_rows.shape[1]
    slots_seq = rows_seq // steps

    def seq_peer(s):
        return (tok, s, kv)

    def own_peer(g):
        return (g // n_kv, seq, lax.rem(g, n_kv))

    barrier = pltpu.get_barrier_semaphore()
    for d in range(1, n_own):
        pl.semaphore_signal(
            barrier, inc=1, device_id=own_peer(lax.rem(own + d, n_own)), device_id_type=MESH
        )
    for d in range(1, n_seq):
        pl.semaphore_signal(
            barrier, inc=1, device_id=seq_peer(lax.rem(seq + d, n_seq)), device_id_type=MESH
        )

    loads = []

    def load(src, dst):
        copy = pltpu.make_async_copy(src, dst, load_sem.at[len(loads)])
        copy.start()
        loads.append(copy)
        return copy

    table_load = load(table_hbm, table)
    wq_load = load(wq_hbm, wq)
    wkv_load = load(wkv_hbm, wkv)
    chunk = 8
    cache_loads = [
        load(cache_hbm.at[pl.ds(c, chunk)], cache.at[pl.ds(c, chunk)])
        for c in range(0, n_req, chunk)
    ]
    wo_load = load(wo_hbm, wo)
    wg_load = load(wg_hbm, wg)
    wu_load = load(wu_hbm, wu)
    wd_load = load(wd_hbm, wd)

    def own_copy(phase, src, dst, g):
        return pltpu.make_async_remote_copy(
            src_ref=src,
            dst_ref=dst,
            send_sem=send_sem.at[phase],
            recv_sem=yc_sem.at[phase, own],
            device_id=own_peer(g),
            device_id_type=MESH,
        )

    def seq_copy(phase, src, dst, s):
        return pltpu.make_async_remote_copy(
            src_ref=src,
            dst_ref=dst,
            send_sem=send_sem.at[phase + 3],
            recv_sem=seq_sem.at[phase, seq],
            device_id=seq_peer(s),
            device_id_type=MESH,
        )

    def own_wait(phase, dst):
        for d in range(1, n_own):
            g = lax.rem(own + d, n_own)
            pltpu.make_async_copy(dst.at[g], dst.at[g], yc_sem.at[phase, g]).wait()

    def seq_wait(phase, dst, s):
        pltpu.make_async_copy(dst.at[s], dst.at[s], seq_sem.at[phase, s]).wait()

    def seq_wait_all(phase, dst):
        for d in range(1, n_seq):
            seq_wait(phase, dst, lax.rem(seq + d, n_seq))

    def sent(index, buffer, count):
        part = buffer.at[pl.ds(0, count)]
        pltpu.make_async_copy(part, part, send_sem.at[index]).wait()

    sub8 = iota((8, 128), 0)

    def ids_block(b, carry):
        value = jnp.zeros((8, 128), jnp.int32)
        for i in range(8):
            request = order_ref[b * 2 + i // steps]
            value = jnp.where(sub8 == i, ids_ref[i % steps, request], value)
        ids_v[pl.ds(pl.multiple_of(b * 8, 8), 8), :] = value
        return carry

    lax.fori_loop(0, n_req * steps // 8, ids_block, 0)

    table_load.wait()
    kt = 512
    n_rows = n_req * steps
    wide_ids = jnp.concatenate([ids_v[...]] * (kt // 128), axis=1) - own * vocab
    lane_k = iota((n_rows, kt), 1)

    def pick(c, acc):
        hot = jnp.where(wide_ids == lane_k + c * kt, 1.0, 0.0).astype(BF16)
        return acc + dot(hot, table[pl.ds(pl.multiple_of(c * kt, kt), kt), :])

    picked = lax.fori_loop(0, vocab // kt, pick, jnp.zeros((n_rows, 128), F32)).astype(BF16)
    x_send[...] = picked.reshape(n_own, rows_own, 128)

    pl.semaphore_wait(barrier, n_own - 1 + n_seq - 1)

    for d in range(1, n_own):
        g = lax.rem(own + d, n_own)
        own_copy(0, x_send.at[g], x_recv.at[own], g).start()
    x_recv[own] = x_send[own]
    own_wait(0, x_recv)
    x_own = x_recv[0].astype(F32)
    for g in range(1, n_own):
        x_own = x_own + x_recv[g].astype(F32)

    x_all[own] = x_own.astype(BF16)
    for d in range(1, n_own):
        g = lax.rem(own + d, n_own)
        own_copy(1, x_all.at[own], x_all.at[own], g).start()
    own_wait(1, x_all)

    per = rows_own // rows_seq

    def seq_rows(s):
        return x_all.at[s // per, pl.ds(pl.multiple_of(lax.rem(s, per) * rows_seq, rows_seq), rows_seq)]

    for d in range(1, n_seq):
        s = lax.rem(seq + d, n_seq)
        seq_copy(0, seq_rows(s), x_rows.at[seq], s).start()
    x_rows[seq] = seq_rows(seq)[...]

    row16 = iota((rows_seq, 128), 0)
    lane16 = iota((rows_seq, 128), 1)
    base_pos = jnp.zeros((rows_seq, 128), jnp.int32)
    for i in range(slots_seq):
        length = len_ref[order_ref[seq * slots_seq + i]]
        base_pos = jnp.where(row16 // steps == i, length, base_pos)
    position = (base_pos + lax.rem(row16, steps)).astype(F32)
    angle = position * freq_ref[...]
    turns = jnp.round(angle * (1.0 / (2.0 * np.pi)))
    angle = angle - turns * 6.28125
    angle = angle - turns * 0.0019350051879882812
    angle = angle - turns * 3.0199159819e-07
    cosine = jnp.cos(angle)
    sine = jnp.sin(angle)
    front = lax.rem(lane16, 64) < 32

    def rotate(v):
        swapped = jnp.where(front, -pltpu.roll(v, 96, 1), pltpu.roll(v, 32, 1))
        return v * cosine + swapped * sine

    seq_wait_all(0, x_rows)
    width = n_seq * 128
    x16 = jnp.concatenate([x_rows[s] for s in range(n_seq)], axis=1).astype(F32)
    inv_attn = lax.rsqrt(jnp.sum(x16 * x16, axis=1, keepdims=True) / width + EPSILON)
    scaled = (x16 * gain_ref[0:1, :]).astype(BF16)
    wq_load.wait()
    wkv_load.wait()
    q_raw = dot(scaled, wq[...]) * inv_attn
    kv_raw = dot(scaled, wkv[...]) * inv_attn
    q_tiles = [rotate(q_raw[:, t * 128 : (t + 1) * 128]).astype(BF16) for t in range(2)]
    low = lane16 < 64
    fresh = jnp.where(low, rotate(kv_raw), kv_raw).astype(BF16).astype(F32)
    q_all[seq] = jnp.concatenate(q_tiles, axis=1)
    for d in range(1, n_seq):
        s = lax.rem(seq + d, n_seq)
        seq_copy(1, q_all.at[seq], q_all.at[seq], s).start()

    key_lo = jnp.where(low, fresh, 0.0)
    val_hi = jnp.where(low, 0.0, fresh)
    keys = [key_lo.astype(BF16), pltpu.roll(key_lo, 64, 1).astype(BF16)]
    values = [pltpu.roll(val_hi, 64, 1).astype(BF16), val_hi.astype(BF16)]
    r_i = iota((rows_seq, rows_seq), 0)
    c_i = iota((rows_seq, rows_seq), 1)
    causal = (r_i // steps == c_i // steps) & (c_i <= r_i)
    f_peak, f_mass, f_acc = [], [], []
    for h in range(4):
        t = jnp.where(causal, dot_nt(q_tiles[h // 2], keys[h % 2]) * 0.125, FLOOR_SCORE)
        peak = jnp.max(t, axis=1, keepdims=True)
        w = jnp.where(causal, jnp.exp(t - peak), 0.0).astype(BF16)
        f_peak.append(peak)
        f_mass.append(jnp.sum(w.astype(F32), axis=1, keepdims=True))
        f_acc.append(dot(w, values[h % 2]))

    for c in cache_loads:
        c.wait()
    seq_wait_all(1, q_all)

    group = 8
    n_group = n_req // group
    pt = 256
    lane_slot = lax.rem(iota((1, 128), 1), group * steps) // steps
    row_slot = lax.rem(iota((128, 128), 0), group * steps) // steps
    lane32 = iota((group * steps, 128), 1)
    value_slot = lax.rem(iota((128, 256), 0), group * steps) // steps

    def attend(k, carry):
        grp = lax.rem(seq // 2 + 1 + k, n_group)
        q32 = q_all[pl.ds(grp * 2, 2)].reshape(group * steps, 256).astype(F32)
        pieces = []
        for h in range(4):
            tile = q32[:, (h // 2) * 128 : (h // 2 + 1) * 128]
            if h % 2:
                tile = pltpu.roll(tile, 64, 1)
            pieces.append(jnp.where(lane32 < 64, tile, 0.0))
        q128 = jnp.concatenate(pieces, axis=0) * 0.125
        requests = [order_ref[grp * group + r] for r in range(group)]
        lengths = jnp.zeros((1, 128), jnp.int32)
        for r in range(group):
            lengths = jnp.where(lane_slot == r, len_ref[requests[r]], lengths)
        lengths = lengths - seq * ctx
        rhs = jnp.concatenate(
            [jnp.where(row_slot == r, q128, 0.0).astype(BF16) for r in range(group)], axis=1
        )
        q_rows[...] = rhs
        peak = jnp.full((1, 128), FLOOR_SCORE, F32)
        for t in range(ctx // pt):
            lhs = jnp.concatenate(
                [cache[requests[r], t * pt : (t + 1) * pt, :] for r in range(group)], axis=1
            )
            scores = dot_nt(lhs, q_rows[...])
            live = iota((pt, 128), 0) + t * pt < lengths
            scores = jnp.where(live, scores, FLOOR_SCORE)
            s_scr[t * pt : (t + 1) * pt, :] = scores
            peak = jnp.maximum(peak, jnp.max(scores, axis=0, keepdims=True))
        mass = jnp.zeros((1, 128), F32)
        for t in range(ctx // pt):
            live = iota((pt, 128), 0) + t * pt < lengths
            w = jnp.exp(s_scr[t * pt : (t + 1) * pt, :] - peak)
            w = jnp.where(live, w, 0.0).astype(BF16)
            mass = mass + jnp.sum(w.astype(F32), axis=0, keepdims=True)
            p_scr[:, t * pt : (t + 1) * pt] = w.T
        total = jnp.zeros((128, 128), F32)
        for r in range(0, group, 2):
            both = jnp.concatenate([cache[requests[r]], cache[requests[r + 1]]], axis=1)
            both = dot(p_scr[...], both)
            total = jnp.where(row_slot == r, both[:, :128], total)
            total = jnp.where(row_slot == r + 1, both[:, 128:], total)
        st_send[grp] = jnp.concatenate([peak, mass], axis=0)
        for pair in range(2):
            even = pltpu.roll(total[pair * 64 : pair * 64 + 32], 64, 1)
            tile = jnp.where(lane32 < 64, even, total[pair * 64 + 32 : pair * 64 + 64])
            for a in range(2):
                acc_send[grp * 2 + a, pair * rows_seq : (pair + 1) * rows_seq] = tile[
                    a * rows_seq : (a + 1) * rows_seq
                ].astype(BF16)
        for a in range(2):
            s = grp * 2 + a

            @pl.when(s != seq)
            def _():
                seq_copy(2, acc_send.at[s], acc_recv.at[seq], s).start()
                seq_copy(3, st_send.at[grp], st_recv.at[seq], s).start()

        return carry

    lax.fori_loop(0, n_group, attend, 0)

    acc_recv[seq] = acc_send[seq]
    st_recv[seq] = st_send[seq // 2]
    seq_wait_all(3, st_recv)
    stats = jnp.concatenate([st_recv[:, 0, :], st_recv[:, 1, :]], axis=0)
    st_t[...] = jnp.concatenate([stats, jnp.zeros((128 - 2 * n_seq, 128), F32)], axis=0).T
    shares, f_share = [], []
    for h in range(4):
        offset = pl.multiple_of(h * 32 + lax.rem(seq, 2) * rows_seq, rows_seq)
        block = st_t[pl.ds(offset, rows_seq), :]
        peaks, masses = block[:, :n_seq], block[:, n_seq : 2 * n_seq]
        top = jnp.maximum(jnp.max(peaks, axis=1, keepdims=True), f_peak[h])
        factor = jnp.exp(peaks - top)
        f_factor = jnp.exp(f_peak[h] - top)
        denom = jnp.sum(factor * masses, axis=1, keepdims=True) + f_factor * f_mass[h]
        shares.append(factor / denom)
        f_share.append(f_factor / denom)
    tiles = []
    for pair in range(2):
        tiles.append(f_acc[2 * pair] * f_share[2 * pair] + f_acc[2 * pair + 1] * f_share[2 * pair + 1])
    seq_wait_all(2, acc_recv)
    for s in range(n_seq):
        part = acc_recv[s].astype(F32)
        for pair in range(2):
            weight = jnp.where(low, shares[2 * pair][:, s : s + 1], shares[2 * pair + 1][:, s : s + 1])
            tiles[pair] = tiles[pair] + weight * part[pair * rows_seq : (pair + 1) * rows_seq]

    at_all[seq] = jnp.concatenate([t.astype(BF16) for t in tiles], axis=1)
    for d in range(1, n_seq):
        s = lax.rem(seq + d, n_seq)
        seq_copy(4, at_all.at[seq], at_all.at[seq], s).start()
    wo_load.wait()
    seq_wait_all(4, at_all)
    partial = dot(at_all[...].reshape(n_rows, 256), wo[...]).astype(BF16)
    o_send[...] = partial.reshape(n_own, rows_own, 128)
    for d in range(1, n_own):
        g = lax.rem(own + d, n_own)
        own_copy(2, o_send.at[g], o_recv.at[own], g).start()
    o_recv[own] = o_send[own]
    own_wait(2, o_recv)
    attn = o_recv[0].astype(F32)
    for g in range(1, n_own):
        attn = attn + o_recv[g].astype(F32)
    mid = (x_own + attn).astype(BF16)
    mid_all[seq] = mid
    for d in range(1, n_seq):
        s = lax.rem(seq + d, n_seq)
        seq_copy(5, mid_all.at[seq], mid_all.at[seq], s).start()

    wg_load.wait()
    wu_load.wait()
    seq_wait_all(5, mid_all)
    m = jnp.concatenate([mid_all[s] for s in range(n_seq)], axis=1).astype(F32)
    inv_mlp = lax.rsqrt(jnp.sum(m * m, axis=1, keepdims=True) / width + EPSILON)
    scaled_mid = (m * gain_ref[1:2, :]).astype(BF16)
    gate = dot(scaled_mid, wg[...]) * inv_mlp
    up = dot(scaled_mid, wu[...]) * inv_mlp
    hidden = (gate / (1.0 + jnp.exp(-gate)) * up).astype(BF16)
    wd_load.wait()
    down = dot(hidden, wd[...]).astype(BF16)
    for s in range(n_seq):
        d_send[s] = down[:, s * 128 : (s + 1) * 128]
    for d in range(1, n_seq):
        s = lax.rem(seq + d, n_seq)
        seq_copy(6, d_send.at[s], d_recv.at[seq], s).start()
    d_recv[seq] = d_send[seq]
    seq_wait_all(6, d_recv)
    result = mid.astype(F32)
    for s in range(n_seq):
        result = result + d_recv[s].astype(F32)
    out_ref[...] = result.astype(BF16).reshape(out_ref.shape)

    sent(0, x_recv, n_own - 1)
    sent(1, x_all, n_own - 1)
    sent(2, o_recv, n_own - 1)
    sent(3, x_rows, n_seq - 1)
    sent(4, q_all, n_seq - 1)
    sent(5, acc_recv, n_seq - 1)
    sent(6, st_recv, n_seq - 1)
    sent(7, at_all, n_seq - 1)
    sent(8, mid_all, n_seq - 1)
    sent(9, d_recv, n_seq - 1)


def solution(mesh):
    n_tok, n_seq, n_kv = mesh.shape["tok"], mesh.shape["seq"], mesh.shape["kv"]
    n_own = n_tok * n_kv
    lanes = np.arange(128) % 32
    freq = (ROPE_BASE ** (-(lanes * 2.0 / 64))).astype(np.float32).reshape(1, 128)

    def per_device(
        token_ids,
        request_order,
        cache_lengths,
        embed_table,
        attn_gain,
        proj_query,
        proj_kv,
        kv_cache,
        proj_out,
        mlp_gain,
        proj_gate,
        proj_up,
        proj_down,
    ):
        n_req, steps = token_ids.shape
        ctx = kv_cache.shape[1]
        rows = n_req * steps
        r_own, r_seq = rows // n_own, rows // n_seq
        width = proj_query.shape[0]
        gains = jnp.stack([attn_gain, mlp_gain]).astype(F32)
        smem = pl.BlockSpec(memory_space=pltpu.SMEM)
        vmem = pl.BlockSpec(memory_space=pltpu.VMEM)
        hbm = pl.BlockSpec(memory_space=pl.ANY)
        weights = [
            embed_table,
            proj_query,
            proj_kv.reshape(width, 128),
            kv_cache.reshape(n_req, ctx, 128),
            proj_out,
            proj_gate,
            proj_up,
            proj_down,
        ]
        scratch = [pltpu.VMEM(w.shape, w.dtype) for w in weights]
        scratch += [
            pltpu.VMEM((rows, 128), jnp.int32),
            pltpu.VMEM((n_own, r_own, 128), BF16),
            pltpu.VMEM((n_own, r_own, 128), BF16),
            pltpu.VMEM((n_own, r_own, 128), BF16),
            pltpu.VMEM((n_seq, r_seq, 128), BF16),
            pltpu.VMEM((n_seq, r_seq, 256), BF16),
            pltpu.VMEM((128, 1024), BF16),
            pltpu.VMEM((ctx, 128), F32),
            pltpu.VMEM((128, ctx), BF16),
            pltpu.VMEM((n_seq, 2 * r_seq, 128), BF16),
            pltpu.VMEM((n_seq, 2 * r_seq, 128), BF16),
            pltpu.VMEM((n_req // 8, 2, 128), F32),
            pltpu.VMEM((n_seq, 2, 128), F32),
            pltpu.VMEM((128, 128), F32),
            pltpu.VMEM((n_seq, r_seq, 256), BF16),
            pltpu.VMEM((n_own, r_own, 128), BF16),
            pltpu.VMEM((n_own, r_own, 128), BF16),
            pltpu.VMEM((n_seq, r_own, 128), BF16),
            pltpu.VMEM((n_seq, r_own, 128), BF16),
            pltpu.VMEM((n_seq, r_own, 128), BF16),
            pltpu.SemaphoreType.DMA((16,)),
            pltpu.SemaphoreType.DMA((10,)),
            pltpu.SemaphoreType.DMA((3, n_own)),
            pltpu.SemaphoreType.DMA((7, n_seq)),
        ]
        return pl.pallas_call(
            functools.partial(layer_kernel, n_tok, n_seq, n_kv),
            out_shape=jax.ShapeDtypeStruct((n_req // n_own, steps, 128), BF16),
            in_specs=[smem, smem, smem, vmem, vmem] + [hbm] * len(weights),
            out_specs=vmem,
            scratch_shapes=scratch,
            compiler_params=pltpu.CompilerParams(
                collective_id=0, has_side_effects=True, vmem_limit_bytes=64 * 1000 * 1000
            ),
            name="layer",
        )(token_ids.T, request_order, cache_lengths, gains, jnp.asarray(freq), *weights)

    placed = (
        P(),
        P(),
        P(),
        P(("tok", "kv"), "seq"),
        P(),
        P(None, ("tok", "kv")),
        P(None, ("tok", "kv"), None),
        P(None, "seq", ("tok", "kv"), None),
        P(("tok", "kv"), "seq"),
        P(),
        P(None, "seq"),
        P(None, "seq"),
        P("seq", None),
    )
    return jax.shard_map(
        per_device,
        mesh=mesh,
        in_specs=placed,
        out_specs=P(("tok", "kv"), None, "seq"),
        check_vma=False,
    )
```

```python
import functools

import jax
import jax.numpy as jnp
import numpy as np
from jax import lax
from jax.experimental import pallas as pl
from jax.experimental.pallas import tpu as pltpu
from jax.sharding import PartitionSpec as P

EPSILON = 1e-05
ROPE_BASE = 1000000.0
FLOOR_SCORE = -1e30
MESH = pl.DeviceIdType.MESH
F32 = jnp.float32
BF16 = jnp.bfloat16


def iota(shape, dim):
    return lax.broadcasted_iota(jnp.int32, shape, dim)


def dot_nt(a, b):
    return lax.dot_general(a, b, (((1,), (1,)), ((), ())), preferred_element_type=F32)


def dot(a, b):
    return jnp.dot(a, b, preferred_element_type=F32)


def interleave(tiles, count, size):
    return jnp.concatenate(
        [t[i * size : (i + 1) * size] for i in range(count) for t in tiles], axis=0
    )


def layer_kernel(
    n_tok,
    n_seq,
    n_kv,
    ids_ref,
    order_ref,
    len_ref,
    gain_ref,
    gain2_ref,
    freq_ref,
    table_hbm,
    wq_hbm,
    wkv_hbm,
    cache_hbm,
    wo_hbm,
    wg_hbm,
    wu_hbm,
    wd_hbm,
    out_ref,
    table,
    wq,
    wkv,
    cache,
    wo,
    wg,
    wu,
    wd,
    keys,
    vals,
    gain2,
    ids_v,
    x_send,
    x_recv,
    x_own_v,
    x_rows,
    q_all,
    s_scr,
    p_scr,
    acc_send,
    acc_recv,
    st_send,
    st_recv,
    st_t,
    at_all,
    o_send,
    o_recv,
    mid_all,
    d_send,
    d_recv,
    load_sem,
    send_sem,
    yc_sem,
    seq_sem,
):
    n_own = n_tok * n_kv
    tok = lax.axis_index("tok")
    seq = lax.axis_index("seq")
    kv = lax.axis_index("kv")
    own = tok * n_kv + kv
    vocab = table.shape[0]
    ctx = cache.shape[1]
    n_req = cache.shape[0]
    steps = 4
    n_rows = n_req * steps
    rows_own = n_rows // n_own
    rows_seq = n_rows // n_seq
    slots_seq = rows_seq // steps
    halves = n_seq // n_own
    width = n_seq * 128

    def seq_peer(s):
        return (tok, s, kv)

    def own_peer(g):
        return (g // n_kv, seq, lax.rem(g, n_kv))

    barrier = pltpu.get_barrier_semaphore()
    for d in range(1, n_own):
        pl.semaphore_signal(
            barrier, inc=1, device_id=own_peer(lax.rem(own + d, n_own)), device_id_type=MESH
        )
    for d in range(1, n_seq):
        pl.semaphore_signal(
            barrier, inc=1, device_id=seq_peer(lax.rem(seq + d, n_seq)), device_id_type=MESH
        )

    loads = []

    def load(src, dst):
        copy = pltpu.make_async_copy(src, dst, load_sem.at[len(loads)])
        copy.start()
        loads.append(copy)
        return copy

    table_load = load(table_hbm, table)
    wq_load = load(wq_hbm, wq)
    wkv_load = load(wkv_hbm, wkv)
    chunk = 8
    cache_loads = [
        load(cache_hbm.at[pl.ds(c, chunk)], cache.at[pl.ds(c, chunk)])
        for c in range(0, n_req, chunk)
    ]
    wo_load = load(wo_hbm, wo)
    wg_load = load(wg_hbm, wg)
    wu_load = load(wu_hbm, wu)
    wd_load = load(wd_hbm, wd)

    def own_copy(phase, src, dst, g):
        return pltpu.make_async_remote_copy(
            src_ref=src,
            dst_ref=dst,
            send_sem=send_sem.at[phase],
            recv_sem=yc_sem.at[phase, own],
            device_id=own_peer(g),
            device_id_type=MESH,
        )

    def seq_copy(phase, src, dst, s):
        return pltpu.make_async_remote_copy(
            src_ref=src,
            dst_ref=dst,
            send_sem=send_sem.at[phase + 3],
            recv_sem=seq_sem.at[phase, seq],
            device_id=seq_peer(s),
            device_id_type=MESH,
        )

    def own_wait(phase, dst):
        for d in range(1, n_own):
            g = lax.rem(own + d, n_own)
            pltpu.make_async_copy(dst.at[g], dst.at[g], yc_sem.at[phase, g]).wait()

    def seq_wait(phase, dst, s):
        pltpu.make_async_copy(dst.at[s], dst.at[s], seq_sem.at[phase, s]).wait()

    def seq_wait_all(phase, dst):
        for d in range(1, n_seq):
            seq_wait(phase, dst, lax.rem(seq + d, n_seq))

    def sent(index, buffer, count):
        part = buffer.at[pl.ds(0, count)]
        pltpu.make_async_copy(part, part, send_sem.at[index]).wait()

    def pair_at(k):
        dz = lax.rem(k // 2, 2) * 2 + k // 4
        return lax.rem(seq // 4 + dz, n_seq // 4) * 2 + lax.rem(seq // 2 + k, 2)

    near = [pair_at(jnp.int32(k)) for k in (0, 1, 4, 5, 6, 7, 2, 3)]

    sub8 = iota((8, 128), 0)

    def ids_block(b, carry):
        value = jnp.zeros((8, 128), jnp.int32)
        for i in range(8):
            request = order_ref[b * 2 + i // steps]
            value = jnp.where(sub8 == i, ids_ref[i % steps, request], value)
        ids_v[pl.ds(pl.multiple_of(b * 8, 8), 8), :] = value
        return carry

    lax.fori_loop(0, n_rows // 8, ids_block, 0)
    gain2[...] = gain2_ref[...].astype(F32)

    table_load.wait()
    kt = 512
    wide_ids = jnp.concatenate([ids_v[...]] * (kt // 128), axis=1) - own * vocab
    lane_k = iota((n_rows, kt), 1)

    def pick(c, acc):
        hot = jnp.where(wide_ids == lane_k + c * kt, 1.0, 0.0).astype(BF16)
        return acc + dot(hot, table[pl.ds(pl.multiple_of(c * kt, kt), kt), :])

    picked = lax.fori_loop(0, vocab // kt, pick, jnp.zeros((n_rows, 128), F32)).astype(BF16)
    x_send[...] = picked.reshape(n_own, rows_own, 128)

    pl.semaphore_wait(barrier, n_own - 1 + n_seq - 1)

    for d in range(1, n_own):
        g = lax.rem(own + d, n_own)
        own_copy(0, x_send.at[g], x_recv.at[own], g).start()
    x_recv[own] = x_send[own]
    own_wait(0, x_recv)
    x_own = x_recv[0].astype(F32)
    for g in range(1, n_own):
        x_own = x_own + x_recv[g].astype(F32)
    x_own_v[...] = x_own.astype(BF16).reshape(halves, rows_seq, 128)

    def x_copy(half, g):
        s = own * halves + half
        return pltpu.make_async_remote_copy(
            src_ref=x_own_v.at[half],
            dst_ref=x_rows.at[seq],
            send_sem=send_sem.at[3],
            recv_sem=seq_sem.at[0, seq],
            device_id=(g // n_kv, s, lax.rem(g, n_kv)),
            device_id_type=MESH,
        )

    holds_own = own == seq // halves
    for half in range(halves):
        for d in range(1, n_own):
            x_copy(half, lax.rem(own + d, n_own)).start()

        @pl.when(own * halves + half != seq)
        def _():
            x_copy(half, own).start()

    @pl.when(holds_own)
    def _():
        x_rows[seq] = x_own_v[lax.rem(seq, halves)]

    for c in cache_loads:
        c.wait()

    def pack(m, carry):
        size = 256
        low = iota((size, 128), 1) < 64
        for t in range(ctx // size):
            a = cache[order_ref[2 * m], t * size : (t + 1) * size, :]
            b = cache[order_ref[2 * m + 1], t * size : (t + 1) * size, :]
            keys[m, t * size : (t + 1) * size, :] = jnp.where(low, a, pltpu.roll(b, 64, 1))
            vals[m, t * size : (t + 1) * size, :] = jnp.where(low, pltpu.roll(a, 64, 1), b)
        return carry

    lax.fori_loop(0, n_req // 2, pack, 0)

    row16 = iota((rows_seq, 128), 0)
    lane16 = iota((rows_seq, 128), 1)
    base_pos = jnp.zeros((rows_seq, 128), jnp.int32)
    for i in range(slots_seq):
        length = len_ref[order_ref[seq * slots_seq + i]]
        base_pos = jnp.where(row16 // steps == i, length, base_pos)
    position = (base_pos + lax.rem(row16, steps)).astype(F32)
    angle = position * freq_ref[...]
    turns = jnp.round(angle * (1.0 / (2.0 * np.pi)))
    angle = angle - turns * 6.28125
    angle = angle - turns * 0.0019350051879882812
    angle = angle - turns * 3.0199159819e-07
    cosine = jnp.cos(angle)
    sine = jnp.sin(angle)
    front = lax.rem(lane16, 64) < 32

    def rotate(v):
        swapped = jnp.where(front, -pltpu.roll(v, 96, 1), pltpu.roll(v, 32, 1))
        return v * cosine + swapped * sine

    gain = jnp.concatenate([gain_ref[s : s + 1, :].astype(F32) for s in range(n_seq)], axis=1)
    wq_load.wait()
    wkv_load.wait()

    for s in range(n_seq):

        @pl.when(jnp.logical_not(holds_own) | (seq != s))
        def _():
            seq_wait(0, x_rows, s)

    x16 = jnp.concatenate([x_rows[s] for s in range(n_seq)], axis=1).astype(F32)
    inv_attn = lax.rsqrt(jnp.sum(x16 * x16, axis=1, keepdims=True) / width + EPSILON)
    scaled = (x16 * gain).astype(BF16)
    q_raw = dot(scaled, wq[...]) * inv_attn
    kv_raw = dot(scaled, wkv[...]) * inv_attn
    q_tiles = [rotate(q_raw[:, t * 128 : (t + 1) * 128]) for t in range(2)]
    query = interleave(q_tiles, slots_seq, steps).astype(BF16)
    q_all[seq] = query
    for k in (6, 7, 2, 3, 4, 5, 1, 0):
        for a in range(2):
            s = near[k] * 2 + a
            if k:
                seq_copy(1, q_all.at[seq], q_all.at[seq], s).start()
            else:

                @pl.when(s != seq)
                def _():
                    seq_copy(1, q_all.at[seq], q_all.at[seq], s).start()

    rows_q = 2 * rows_seq
    low16 = lane16 < 64
    low32 = iota((rows_q, 128), 1) < 64
    fresh = jnp.where(low16, rotate(kv_raw), kv_raw).astype(BF16).astype(F32)
    key_lo = jnp.where(low16, fresh, 0.0)
    val_hi = jnp.where(low16, 0.0, fresh)
    f_keys = [key_lo.astype(BF16), pltpu.roll(key_lo, 64, 1).astype(BF16)]
    f_vals = [pltpu.roll(val_hi, 64, 1).astype(BF16), val_hi.astype(BF16)]
    r_i = iota((rows_q, rows_seq), 0)
    c_i = iota((rows_q, rows_seq), 1)
    causal = (r_i // (2 * steps) == c_i // steps) & (lax.rem(c_i, steps) <= lax.rem(r_i, steps))
    f_peak, f_mass, f_acc = [], [], []
    for hb in range(2):
        t = jnp.where(causal, dot_nt(query, f_keys[hb]) * 0.125, FLOOR_SCORE)
        peak = jnp.max(t, axis=1, keepdims=True)
        w = jnp.where(causal, jnp.exp(t - peak), 0.0).astype(BF16)
        f_peak.append(peak)
        f_mass.append(jnp.sum(w.astype(F32), axis=1, keepdims=True))
        f_acc.append(dot(w, f_vals[hb]))

    group = 8
    n_group = n_req // group
    pt = 512
    lane_slot = iota((1, 128), 1) // 16
    low8 = iota((8, 128), 1) < 64

    def attend(k, carry):
        grp = pair_at(k)
        for a in range(2):
            s = grp * 2 + a

            @pl.when(s != seq)
            def _():
                seq_wait(1, q_all, s)

        q64 = q_all[pl.ds(grp * 2, 2)].reshape(2 * rows_q, 128).astype(F32) * 0.125
        r64 = pltpu.roll(q64, 64, 1)
        zero = jnp.zeros((32, 128), F32)
        columns = []
        for m in range(group // 2):
            e, o = slice(16 * m, 16 * m + 8), slice(16 * m + 8, 16 * m + 16)
            block = jnp.concatenate(
                [
                    jnp.where(low8, q64[e], 0.0),
                    jnp.where(low8, r64[e], 0.0),
                    jnp.where(low8, 0.0, r64[o]),
                    jnp.where(low8, 0.0, q64[o]),
                ],
                axis=0,
            )
            columns.append(
                jnp.concatenate([block if i == m else zero for i in range(group // 2)], axis=0)
            )
        rhs = jnp.concatenate(columns, axis=1).astype(BF16)
        lengths = jnp.zeros((1, 128), jnp.int32)
        for r in range(group):
            lengths = jnp.where(lane_slot == r, len_ref[order_ref[grp * group + r]], lengths)
        lengths = lengths - seq * ctx
        peak = jnp.full((1, 128), FLOOR_SCORE, F32)
        for t in range(ctx // pt):
            lhs = jnp.concatenate(
                [keys[grp * 4 + m, t * pt : (t + 1) * pt, :] for m in range(group // 2)], axis=1
            )
            live = iota((pt, 128), 0) + t * pt < lengths
            scores = jnp.where(live, dot_nt(lhs, rhs), FLOOR_SCORE)
            s_scr[t * pt : (t + 1) * pt, :] = scores
            peak = jnp.maximum(peak, jnp.max(scores, axis=0, keepdims=True))
        mass = jnp.zeros((1, 128), F32)
        for t in range(ctx // pt):
            live = iota((pt, 128), 0) + t * pt < lengths
            w = jnp.exp(s_scr[t * pt : (t + 1) * pt, :] - peak)
            w = jnp.where(live, w, 0.0).astype(BF16)
            mass = mass + jnp.sum(w.astype(F32), axis=0, keepdims=True)
            p_scr[:, t * pt : (t + 1) * pt] = w.T
        st_send[grp] = jnp.concatenate([peak, mass], axis=0)
        for a in range(2):
            both = jnp.concatenate([vals[grp * 4 + 2 * a], vals[grp * 4 + 2 * a + 1]], axis=1)
            total = dot(p_scr[a * 64 : (a + 1) * 64, :], both)
            pieces = []
            for i in range(slots_seq):
                tile = total[16 * i : 16 * i + 16, (i // 2) * 128 : (i // 2 + 1) * 128]
                if i % 2:
                    pieces.append(jnp.where(low8, pltpu.roll(tile[:8], 64, 1), tile[8:]))
                else:
                    pieces.append(jnp.where(low8, tile[:8], pltpu.roll(tile[8:], 64, 1)))
            s = grp * 2 + a
            acc_send[s] = jnp.concatenate(pieces, axis=0).astype(BF16)

            @pl.when(s != seq)
            def _():
                seq_copy(3, st_send.at[grp], st_recv.at[seq], s).start()
                seq_copy(2, acc_send.at[s], acc_recv.at[seq], s).start()

        return carry

    lax.fori_loop(0, n_group, attend, 0)

    acc_recv[seq] = acc_send[seq]
    st_recv[seq] = st_send[seq // 2]
    seq_wait_all(3, st_recv)
    stats = jnp.concatenate([st_recv[:, 0, :], st_recv[:, 1, :]], axis=0)
    st_t[...] = jnp.concatenate([stats, jnp.zeros((128 - 2 * n_seq, 128), F32)], axis=0).T
    mine = st_t[pl.ds(pl.multiple_of(lax.rem(seq, 2) * 64, 64), 64), :]
    shares, f_share = [], []
    for hb in range(2):
        block = jnp.concatenate(
            [mine[16 * i + 8 * hb : 16 * i + 8 * hb + 8] for i in range(slots_seq)], axis=0
        )
        peaks, masses = block[:, :n_seq], block[:, n_seq : 2 * n_seq]
        top = jnp.maximum(jnp.max(peaks, axis=1, keepdims=True), f_peak[hb])
        factor = jnp.exp(peaks - top)
        f_factor = jnp.exp(f_peak[hb] - top)
        denom = jnp.sum(factor * masses, axis=1, keepdims=True) + f_factor * f_mass[hb]
        shares.append(factor / denom)
        f_share.append(f_factor / denom)
    weights = [jnp.where(low32, shares[0][:, s : s + 1], shares[1][:, s : s + 1]) for s in range(n_seq)]
    attended = f_acc[0] * f_share[0] + f_acc[1] * f_share[1]
    seq_wait_all(2, acc_recv)
    for s in range(n_seq):
        attended = attended + weights[s] * acc_recv[s].astype(F32)

    at_rows = [
        jnp.concatenate(
            [attended[8 * i + 4 * t : 8 * i + 4 * t + 4] for i in range(slots_seq)], axis=0
        )
        for t in range(2)
    ]
    at_all[seq] = jnp.concatenate(at_rows, axis=1).astype(BF16)
    for k in (6, 7, 2, 3, 4, 5, 1, 0):
        for a in range(2):
            s = near[k] * 2 + a
            if k:
                seq_copy(4, at_all.at[seq], at_all.at[seq], s).start()
            else:

                @pl.when(s != seq)
                def _():
                    seq_copy(4, at_all.at[seq], at_all.at[seq], s).start()
    wo_load.wait()
    seq_wait_all(4, at_all)
    partial = dot(at_all[...].reshape(n_rows, 256), wo[...]).astype(BF16)
    o_send[...] = partial.reshape(n_own, rows_own, 128)
    for d in range(1, n_own):
        g = lax.rem(own + d, n_own)
        own_copy(2, o_send.at[g], o_recv.at[own], g).start()
    o_recv[own] = o_send[own]
    own_wait(2, o_recv)
    attn = o_recv[0].astype(F32)
    for g in range(1, n_own):
        attn = attn + o_recv[g].astype(F32)
    mid = (x_own + attn).astype(BF16)
    mid_all[seq] = mid
    for k in (6, 7, 2, 3, 4, 5, 1, 0):
        for a in range(2):
            s = near[k] * 2 + a
            if k:
                seq_copy(5, mid_all.at[seq], mid_all.at[seq], s).start()
            else:

                @pl.when(s != seq)
                def _():
                    seq_copy(5, mid_all.at[seq], mid_all.at[seq], s).start()

    wg_load.wait()
    wu_load.wait()
    wd_load.wait()
    ff = wg.shape[1]
    gate = jnp.zeros((rows_own, ff), F32)
    up = jnp.zeros((rows_own, ff), F32)
    squares = jnp.zeros((rows_own, 128), F32)
    for k in range(n_seq // 2):
        pair = near[k]
        parts = []
        for a in range(2):
            s = pair * 2 + a
            if k:
                seq_wait(5, mid_all, s)
            else:

                @pl.when(s != seq)
                def _():
                    seq_wait(5, mid_all, s)

            m = mid_all[s].astype(F32)
            squares = squares + m * m
            parts.append((m * gain2[pl.ds(s, 1), :]).astype(BF16))
        both = jnp.concatenate(parts, axis=1)
        rows = pl.ds(pl.multiple_of(pair * 256, 256), 256)
        gate = gate + dot(both, wg[rows, :])
        up = up + dot(both, wu[rows, :])
    inv_mlp = lax.rsqrt(jnp.sum(squares, axis=1, keepdims=True) / width + EPSILON)
    gate = gate * inv_mlp
    hidden = (gate / (1.0 + jnp.exp(-gate)) * (up * inv_mlp)).astype(BF16)
    for k in (6, 7, 2, 3, 4, 5, 1, 0):
        pair = near[k]
        down = dot(hidden, wd[:, pl.ds(pl.multiple_of(pair * 256, 256), 256)]).astype(BF16)
        for a in range(2):
            s = pair * 2 + a
            d_send[s] = down[:, a * 128 : (a + 1) * 128]
            if k:
                seq_copy(6, d_send.at[s], d_recv.at[seq], s).start()
            else:

                @pl.when(s != seq)
                def _():
                    seq_copy(6, d_send.at[s], d_recv.at[seq], s).start()

    d_recv[seq] = d_send[seq]
    seq_wait_all(6, d_recv)
    result = mid.astype(F32)
    for s in range(n_seq):
        result = result + d_recv[s].astype(F32)
    out_ref[...] = result.astype(BF16).reshape(out_ref.shape)

    sent(0, x_recv, n_own - 1)
    sent(2, o_recv, n_own - 1)
    sent(3, x_rows, n_seq - 1)

    @pl.when(jnp.logical_not(holds_own))
    def _():
        sent(3, x_rows, 1)

    sent(4, q_all, n_seq - 1)
    sent(5, acc_recv, n_seq - 1)
    sent(6, st_recv, n_seq - 1)
    sent(7, at_all, n_seq - 1)
    sent(8, mid_all, n_seq - 1)
    sent(9, d_recv, n_seq - 1)


def solution(mesh):
    n_tok, n_seq, n_kv = mesh.shape["tok"], mesh.shape["seq"], mesh.shape["kv"]
    n_own = n_tok * n_kv
    lanes = np.arange(128) % 32
    freq = (ROPE_BASE ** (-(lanes * 2.0 / 64))).astype(np.float32).reshape(1, 128)

    def per_device(
        token_ids,
        request_order,
        cache_lengths,
        embed_table,
        attn_gain,
        proj_query,
        proj_kv,
        kv_cache,
        proj_out,
        mlp_gain,
        proj_gate,
        proj_up,
        proj_down,
    ):
        n_req, steps = token_ids.shape
        ctx = kv_cache.shape[1]
        rows = n_req * steps
        r_own, r_seq = rows // n_own, rows // n_seq
        width = proj_query.shape[0]
        smem = pl.BlockSpec(memory_space=pltpu.SMEM)
        vmem = pl.BlockSpec(memory_space=pltpu.VMEM)
        hbm = pl.BlockSpec(memory_space=pl.ANY)
        weights = [
            embed_table,
            proj_query,
            proj_kv.reshape(width, 128),
            kv_cache.reshape(n_req, ctx, 128),
            proj_out,
            proj_gate,
            proj_up,
            proj_down,
        ]
        scratch = [pltpu.VMEM(w.shape, w.dtype) for w in weights]
        scratch += [
            pltpu.VMEM((n_req // 2, ctx, 128), BF16),
            pltpu.VMEM((n_req // 2, ctx, 128), BF16),
            pltpu.VMEM((n_seq, 128), F32),
            pltpu.VMEM((rows, 128), jnp.int32),
            pltpu.VMEM((n_own, r_own, 128), BF16),
            pltpu.VMEM((n_own, r_own, 128), BF16),
            pltpu.VMEM((n_seq // n_own, r_seq, 128), BF16),
            pltpu.VMEM((n_seq, r_seq, 128), BF16),
            pltpu.VMEM((n_seq, 2 * r_seq, 128), BF16),
            pltpu.VMEM((ctx, 128), F32),
            pltpu.VMEM((128, ctx), BF16),
            pltpu.VMEM((n_seq, 2 * r_seq, 128), BF16),
            pltpu.VMEM((n_seq, 2 * r_seq, 128), BF16),
            pltpu.VMEM((n_req // 8, 2, 128), F32),
            pltpu.VMEM((n_seq, 2, 128), F32),
            pltpu.VMEM((128, 128), F32),
            pltpu.VMEM((n_seq, r_seq, 256), BF16),
            pltpu.VMEM((n_own, r_own, 128), BF16),
            pltpu.VMEM((n_own, r_own, 128), BF16),
            pltpu.VMEM((n_seq, r_own, 128), BF16),
            pltpu.VMEM((n_seq, r_own, 128), BF16),
            pltpu.VMEM((n_seq, r_own, 128), BF16),
            pltpu.SemaphoreType.DMA((16,)),
            pltpu.SemaphoreType.DMA((10,)),
            pltpu.SemaphoreType.DMA((3, n_own)),
            pltpu.SemaphoreType.DMA((7, n_seq)),
        ]
        return pl.pallas_call(
            functools.partial(layer_kernel, n_tok, n_seq, n_kv),
            out_shape=jax.ShapeDtypeStruct((n_req // n_own, steps, 128), BF16),
            in_specs=[smem, smem, smem, vmem, vmem, vmem] + [hbm] * len(weights),
            out_specs=vmem,
            scratch_shapes=scratch,
            compiler_params=pltpu.CompilerParams(
                collective_id=0, has_side_effects=True, vmem_limit_bytes=64 * 1000 * 1000
            ),
            name="layer",
        )(
            token_ids.T,
            request_order,
            cache_lengths,
            attn_gain.reshape(n_seq, 128),
            mlp_gain.reshape(n_seq, 128),
            jnp.asarray(freq),
            *weights,
        )

    placed = (
        P(),
        P(),
        P(),
        P(("tok", "kv"), "seq"),
        P(),
        P(None, ("tok", "kv")),
        P(None, ("tok", "kv"), None),
        P(None, "seq", ("tok", "kv"), None),
        P(("tok", "kv"), "seq"),
        P(),
        P(None, "seq"),
        P(None, "seq"),
        P("seq", None),
    )
    return jax.shard_map(
        per_device,
        mesh=mesh,
        in_specs=placed,
        out_specs=P(("tok", "kv"), None, "seq"),
        check_vma=False,
    )
```

```python
import functools

import jax
import jax.numpy as jnp
import numpy as np
from jax import lax
from jax.experimental import pallas as pl
from jax.experimental.pallas import tpu as pltpu
from jax.sharding import PartitionSpec as P

EPSILON = 1e-05
ROPE_BASE = 1000000.0
FLOOR_SCORE = -1e30
MESH = pl.DeviceIdType.MESH
F32 = jnp.float32
BF16 = jnp.bfloat16


def iota(shape, dim):
    return lax.broadcasted_iota(jnp.int32, shape, dim)


def dot_nt(a, b):
    return lax.dot_general(a, b, (((1,), (1,)), ((), ())), preferred_element_type=F32)


def dot(a, b):
    return jnp.dot(a, b, preferred_element_type=F32)


def interleave(tiles, count, size):
    return jnp.concatenate(
        [t[i * size : (i + 1) * size] for i in range(count) for t in tiles], axis=0
    )


def layer_kernel(
    n_tok,
    n_seq,
    n_kv,
    ids_ref,
    order_ref,
    len_ref,
    gain_ref,
    gain2_ref,
    freq_ref,
    table_hbm,
    wq_hbm,
    wkv_hbm,
    cache_hbm,
    wo_hbm,
    wg_hbm,
    wu_hbm,
    wd_hbm,
    out_ref,
    table,
    wq,
    wkv,
    cache,
    wo,
    wg,
    wu,
    wd,
    keys,
    gain2,
    ids_v,
    x_send,
    x_recv,
    x_own_v,
    x_rows,
    q_all,
    s_even,
    s_odd,
    p_even,
    p_odd,
    acc_send,
    acc_recv,
    st_send,
    st_recv,
    st_t,
    at_all,
    o_send,
    o_recv,
    mid_all,
    d_send,
    d_recv,
    load_sem,
    send_sem,
    yc_sem,
    seq_sem,
):
    n_own = n_tok * n_kv
    tok = lax.axis_index("tok")
    seq = lax.axis_index("seq")
    kv = lax.axis_index("kv")
    own = tok * n_kv + kv
    vocab = table.shape[0]
    ctx = cache.shape[1]
    n_req = cache.shape[0]
    steps = 4
    n_rows = n_req * steps
    rows_own = n_rows // n_own
    rows_seq = n_rows // n_seq
    slots_seq = rows_seq // steps
    halves = n_seq // n_own
    width = n_seq * 128

    def seq_peer(s):
        return (tok, s, kv)

    def own_peer(g):
        return (g // n_kv, seq, lax.rem(g, n_kv))

    barrier = pltpu.get_barrier_semaphore()
    for d in range(1, n_own):
        pl.semaphore_signal(
            barrier, inc=1, device_id=own_peer(lax.rem(own + d, n_own)), device_id_type=MESH
        )
    for d in range(1, n_seq):
        pl.semaphore_signal(
            barrier, inc=1, device_id=seq_peer(lax.rem(seq + d, n_seq)), device_id_type=MESH
        )

    loads = []

    def load(src, dst):
        copy = pltpu.make_async_copy(src, dst, load_sem.at[len(loads)])
        copy.start()
        loads.append(copy)
        return copy

    table_load = load(table_hbm, table)
    wq_load = load(wq_hbm, wq)
    wkv_load = load(wkv_hbm, wkv)
    chunk = 8
    cache_loads = [
        load(cache_hbm.at[pl.ds(c, chunk)], cache.at[pl.ds(c, chunk)])
        for c in range(0, n_req, chunk)
    ]
    wo_load = load(wo_hbm, wo)
    wg_load = load(wg_hbm, wg)
    wu_load = load(wu_hbm, wu)
    wd_load = load(wd_hbm, wd)

    def own_copy(phase, src, dst, g):
        return pltpu.make_async_remote_copy(
            src_ref=src,
            dst_ref=dst,
            send_sem=send_sem.at[phase],
            recv_sem=yc_sem.at[phase, own],
            device_id=own_peer(g),
            device_id_type=MESH,
        )

    def seq_copy(phase, src, dst, s):
        return pltpu.make_async_remote_copy(
            src_ref=src,
            dst_ref=dst,
            send_sem=send_sem.at[phase + 3],
            recv_sem=seq_sem.at[phase, seq],
            device_id=seq_peer(s),
            device_id_type=MESH,
        )

    def own_wait(phase, dst):
        for d in range(1, n_own):
            g = lax.rem(own + d, n_own)
            pltpu.make_async_copy(dst.at[g], dst.at[g], yc_sem.at[phase, g]).wait()

    def seq_wait(phase, dst, s):
        pltpu.make_async_copy(dst.at[s], dst.at[s], seq_sem.at[phase, s]).wait()

    def seq_wait_all(phase, dst):
        for d in range(1, n_seq):
            seq_wait(phase, dst, lax.rem(seq + d, n_seq))

    def sent(index, buffer, count):
        part = buffer.at[pl.ds(0, count)]
        pltpu.make_async_copy(part, part, send_sem.at[index]).wait()

    def pair_at(k):
        dz = lax.rem(k // 2, 2) * 2 + k // 4
        return lax.rem(seq // 4 + dz, n_seq // 4) * 2 + lax.rem(seq // 2 + k, 2)

    near = [pair_at(jnp.int32(k)) for k in (0, 1, 4, 5, 6, 7, 2, 3)]

    sub8 = iota((8, 128), 0)

    def ids_block(b, carry):
        value = jnp.zeros((8, 128), jnp.int32)
        for i in range(8):
            request = order_ref[b * 2 + i // steps]
            value = jnp.where(sub8 == i, ids_ref[i % steps, request], value)
        ids_v[pl.ds(pl.multiple_of(b * 8, 8), 8), :] = value
        return carry

    lax.fori_loop(0, n_rows // 8, ids_block, 0)
    gain2[...] = gain2_ref[...].astype(F32)

    table_load.wait()
    kt = 512
    wide_ids = jnp.concatenate([ids_v[...]] * (kt // 128), axis=1) - own * vocab
    lane_k = iota((n_rows, kt), 1)

    def pick(c, acc):
        hot = jnp.where(wide_ids == lane_k + c * kt, 1.0, 0.0).astype(BF16)
        return acc + dot(hot, table[pl.ds(pl.multiple_of(c * kt, kt), kt), :])

    picked = lax.fori_loop(0, vocab // kt, pick, jnp.zeros((n_rows, 128), F32)).astype(BF16)
    x_send[...] = picked.reshape(n_own, rows_own, 128)

    pl.semaphore_wait(barrier, n_own - 1 + n_seq - 1)

    for d in range(1, n_own):
        g = lax.rem(own + d, n_own)
        own_copy(0, x_send.at[g], x_recv.at[own], g).start()
    x_recv[own] = x_send[own]
    own_wait(0, x_recv)
    x_own = x_recv[0].astype(F32)
    for g in range(1, n_own):
        x_own = x_own + x_recv[g].astype(F32)
    x_own_v[...] = x_own.astype(BF16).reshape(halves, rows_seq, 128)

    def x_copy(half, g):
        s = own * halves + half
        return pltpu.make_async_remote_copy(
            src_ref=x_own_v.at[half],
            dst_ref=x_rows.at[seq],
            send_sem=send_sem.at[3],
            recv_sem=seq_sem.at[0, seq],
            device_id=(g // n_kv, s, lax.rem(g, n_kv)),
            device_id_type=MESH,
        )

    holds_own = own == seq // halves
    for half in range(halves):
        for d in range(1, n_own):
            x_copy(half, lax.rem(own + d, n_own)).start()

        @pl.when(own * halves + half != seq)
        def _():
            x_copy(half, own).start()

    @pl.when(holds_own)
    def _():
        x_rows[seq] = x_own_v[lax.rem(seq, halves)]

    for c in cache_loads:
        c.wait()

    def pack(m, carry):
        size = 256
        low = iota((size, 128), 1) < 64
        for t in range(ctx // size):
            a = cache[order_ref[2 * m], t * size : (t + 1) * size, :]
            b = cache[order_ref[2 * m + 1], t * size : (t + 1) * size, :]
            keys[m, t * size : (t + 1) * size, :] = jnp.where(low, a, pltpu.roll(b, 64, 1))
        return carry

    lax.fori_loop(0, n_req // 2, pack, 0)

    row16 = iota((rows_seq, 128), 0)
    lane16 = iota((rows_seq, 128), 1)
    base_pos = jnp.zeros((rows_seq, 128), jnp.int32)
    for i in range(slots_seq):
        length = len_ref[order_ref[seq * slots_seq + i]]
        base_pos = jnp.where(row16 // steps == i, length, base_pos)
    position = (base_pos + lax.rem(row16, steps)).astype(F32)
    angle = position * freq_ref[...]
    turns = jnp.round(angle * (1.0 / (2.0 * np.pi)))
    angle = angle - turns * 6.28125
    angle = angle - turns * 0.0019350051879882812
    angle = angle - turns * 3.0199159819e-07
    cosine = jnp.cos(angle)
    sine = jnp.sin(angle)
    front = lax.rem(lane16, 64) < 32

    def rotate(v):
        swapped = jnp.where(front, -pltpu.roll(v, 96, 1), pltpu.roll(v, 32, 1))
        return v * cosine + swapped * sine

    gain = jnp.concatenate([gain_ref[s : s + 1, :].astype(F32) for s in range(n_seq)], axis=1)
    wq_load.wait()
    wkv_load.wait()

    for s in range(n_seq):

        @pl.when(jnp.logical_not(holds_own) | (seq != s))
        def _():
            seq_wait(0, x_rows, s)

    x16 = jnp.concatenate([x_rows[s] for s in range(n_seq)], axis=1).astype(F32)
    inv_attn = lax.rsqrt(jnp.sum(x16 * x16, axis=1, keepdims=True) / width + EPSILON)
    scaled = (x16 * gain).astype(BF16)
    q_raw = dot(scaled, wq[...]) * inv_attn
    kv_raw = dot(scaled, wkv[...]) * inv_attn
    q_tiles = [rotate(q_raw[:, t * 128 : (t + 1) * 128]) for t in range(2)]
    query = interleave(q_tiles, slots_seq, steps).astype(BF16)
    q_all[seq] = query
    for k in (6, 7, 2, 3, 4, 5, 1, 0):
        for a in range(2):
            s = near[k] * 2 + a
            if k:
                seq_copy(1, q_all.at[seq], q_all.at[seq], s).start()
            else:

                @pl.when(s != seq)
                def _():
                    seq_copy(1, q_all.at[seq], q_all.at[seq], s).start()

    rows_q = 2 * rows_seq
    low16 = lane16 < 64
    low32 = iota((rows_q, 128), 1) < 64
    fresh = jnp.where(low16, rotate(kv_raw), kv_raw).astype(BF16).astype(F32)
    key_lo = jnp.where(low16, fresh, 0.0)
    val_hi = jnp.where(low16, 0.0, fresh)
    f_keys = [key_lo.astype(BF16), pltpu.roll(key_lo, 64, 1).astype(BF16)]
    f_vals = [pltpu.roll(val_hi, 64, 1).astype(BF16), val_hi.astype(BF16)]
    r_i = iota((rows_q, rows_seq), 0)
    c_i = iota((rows_q, rows_seq), 1)
    causal = (r_i // (2 * steps) == c_i // steps) & (lax.rem(c_i, steps) <= lax.rem(r_i, steps))
    f_peak, f_mass, f_acc = [], [], []
    for hb in range(2):
        t = jnp.where(causal, dot_nt(query, f_keys[hb]) * 0.125, FLOOR_SCORE)
        peak = jnp.max(t, axis=1, keepdims=True)
        w = jnp.where(causal, jnp.exp(t - peak), 0.0).astype(BF16)
        f_peak.append(peak)
        f_mass.append(jnp.sum(w.astype(F32), axis=1, keepdims=True))
        f_acc.append(dot(w, f_vals[hb]))

    group = 8
    n_group = n_req // group
    pt = 512
    lane_slot = iota((1, 128), 1) // 16
    low8 = iota((8, 128), 1) < 64

    def arrive(k):
        for a in range(2):
            s = pair_at(k) * 2 + a

            @pl.when(s != seq)
            def _():
                seq_wait(1, q_all, s)

    def score(k, s_scr):
        grp = pair_at(k)
        q64 = q_all[pl.ds(grp * 2, 2)].reshape(2 * rows_q, 128).astype(F32) * 0.125
        r64 = pltpu.roll(q64, 64, 1)
        zero = jnp.zeros((32, 128), F32)
        columns = []
        for m in range(group // 2):
            e, o = slice(16 * m, 16 * m + 8), slice(16 * m + 8, 16 * m + 16)
            block = jnp.concatenate(
                [
                    jnp.where(low8, q64[e], 0.0),
                    jnp.where(low8, r64[e], 0.0),
                    jnp.where(low8, 0.0, r64[o]),
                    jnp.where(low8, 0.0, q64[o]),
                ],
                axis=0,
            )
            columns.append(
                jnp.concatenate([block if i == m else zero for i in range(group // 2)], axis=0)
            )
        rhs = jnp.concatenate(columns, axis=1).astype(BF16)
        lengths = jnp.zeros((1, 128), jnp.int32)
        for r in range(group):
            lengths = jnp.where(lane_slot == r, len_ref[order_ref[grp * group + r]], lengths)
        lengths = lengths - seq * ctx
        peak = jnp.full((1, 128), FLOOR_SCORE, F32)
        for t in range(ctx // pt):
            lhs = jnp.concatenate(
                [keys[grp * 4 + m, t * pt : (t + 1) * pt, :] for m in range(group // 2)], axis=1
            )
            live = iota((pt, 128), 0) + t * pt < lengths
            scores = jnp.where(live, dot_nt(lhs, rhs), FLOOR_SCORE)
            s_scr[t * pt : (t + 1) * pt, :] = scores
            peak = jnp.maximum(peak, jnp.max(scores, axis=0, keepdims=True))
        return peak, lengths

    def weigh(k, s_scr, p_scr, peak, lengths):
        grp = pair_at(k)
        shift = jnp.where(lengths > 0, peak, 0.0)
        mass = jnp.zeros((1, 128), F32)
        for t in range(ctx // pt):
            w = jnp.exp(s_scr[t * pt : (t + 1) * pt, :] - shift).astype(BF16)
            mass = mass + jnp.sum(w.astype(F32), axis=0, keepdims=True)
            p_scr[:, t * pt : (t + 1) * pt] = w.T
        st_send[grp] = jnp.concatenate([peak, mass], axis=0)
        for a in range(2):
            pieces = []
            for i in range(0, slots_seq, 2):
                r = a * slots_seq + i
                both = jnp.concatenate(
                    [cache[order_ref[grp * group + r + e]] for e in range(2)], axis=1
                )
                total = dot(p_scr[r * 16 : r * 16 + 32, :], both)
                for e in range(2):
                    tile = total[16 * e : 16 * e + 16, e * 128 : e * 128 + 128]
                    pieces.append(jnp.where(low8, pltpu.roll(tile[:8], 64, 1), tile[8:]))
            acc_send[grp * 2 + a] = jnp.concatenate(pieces, axis=0).astype(BF16)

    def deliver(k):
        grp = pair_at(k)
        for a in range(2):
            s = grp * 2 + a

            @pl.when(s != seq)
            def _():
                seq_copy(3, st_send.at[grp], st_recv.at[seq], s).start()
                seq_copy(2, acc_send.at[s], acc_recv.at[seq], s).start()

    def attend(i, carry):
        arrive(2 * i + 1)
        following = score(2 * i + 1, s_odd)
        weigh(2 * i, s_even, p_even, *carry)
        deliver(2 * i)
        arrive(2 * i + 2)
        carry = score(2 * i + 2, s_even)
        weigh(2 * i + 1, s_odd, p_odd, *following)
        deliver(2 * i + 1)
        return carry

    arrive(jnp.int32(0))
    carry = lax.fori_loop(0, n_group // 2 - 1, attend, score(jnp.int32(0), s_even))
    last = jnp.int32(n_group - 2)
    arrive(last + 1)
    following = score(last + 1, s_odd)
    weigh(last, s_even, p_even, *carry)
    deliver(last)
    weigh(last + 1, s_odd, p_odd, *following)
    deliver(last + 1)

    acc_recv[seq] = acc_send[seq]
    st_recv[seq] = st_send[seq // 2]
    seq_wait_all(3, st_recv)
    stats = jnp.concatenate([st_recv[:, 0, :], st_recv[:, 1, :]], axis=0)
    st_t[...] = jnp.concatenate([stats, jnp.zeros((128 - 2 * n_seq, 128), F32)], axis=0).T
    mine = st_t[pl.ds(pl.multiple_of(lax.rem(seq, 2) * 64, 64), 64), :]
    shares, f_share = [], []
    for hb in range(2):
        block = jnp.concatenate(
            [mine[16 * i + 8 * hb : 16 * i + 8 * hb + 8] for i in range(slots_seq)], axis=0
        )
        peaks, masses = block[:, :n_seq], block[:, n_seq : 2 * n_seq]
        top = jnp.maximum(jnp.max(peaks, axis=1, keepdims=True), f_peak[hb])
        factor = jnp.exp(peaks - top)
        f_factor = jnp.exp(f_peak[hb] - top)
        denom = jnp.sum(factor * masses, axis=1, keepdims=True) + f_factor * f_mass[hb]
        shares.append(factor / denom)
        f_share.append(f_factor / denom)
    weights = [jnp.where(low32, shares[0][:, s : s + 1], shares[1][:, s : s + 1]) for s in range(n_seq)]
    attended = f_acc[0] * f_share[0] + f_acc[1] * f_share[1]
    seq_wait_all(2, acc_recv)
    for s in range(n_seq):
        attended = attended + weights[s] * acc_recv[s].astype(F32)

    at_rows = [
        jnp.concatenate(
            [attended[8 * i + 4 * t : 8 * i + 4 * t + 4] for i in range(slots_seq)], axis=0
        )
        for t in range(2)
    ]
    at_all[seq] = jnp.concatenate(at_rows, axis=1).astype(BF16)
    for k in (6, 7, 2, 3, 4, 5, 1, 0):
        for a in range(2):
            s = near[k] * 2 + a
            if k:
                seq_copy(4, at_all.at[seq], at_all.at[seq], s).start()
            else:

                @pl.when(s != seq)
                def _():
                    seq_copy(4, at_all.at[seq], at_all.at[seq], s).start()
    wo_load.wait()
    seq_wait_all(4, at_all)
    partial = dot(at_all[...].reshape(n_rows, 256), wo[...]).astype(BF16)
    o_send[...] = partial.reshape(n_own, rows_own, 128)
    for d in range(1, n_own):
        g = lax.rem(own + d, n_own)
        own_copy(2, o_send.at[g], o_recv.at[own], g).start()
    o_recv[own] = o_send[own]
    own_wait(2, o_recv)
    attn = o_recv[0].astype(F32)
    for g in range(1, n_own):
        attn = attn + o_recv[g].astype(F32)
    mid = (x_own + attn).astype(BF16)
    mid_all[seq] = mid
    for k in (6, 7, 2, 3, 4, 5, 1, 0):
        for a in range(2):
            s = near[k] * 2 + a
            if k:
                seq_copy(5, mid_all.at[seq], mid_all.at[seq], s).start()
            else:

                @pl.when(s != seq)
                def _():
                    seq_copy(5, mid_all.at[seq], mid_all.at[seq], s).start()

    wg_load.wait()
    wu_load.wait()
    wd_load.wait()
    ff = wg.shape[1]
    gate = jnp.zeros((rows_own, ff), F32)
    up = jnp.zeros((rows_own, ff), F32)
    squares = jnp.zeros((rows_own, 128), F32)
    for k in range(n_seq // 2):
        pair = near[k]
        parts = []
        for a in range(2):
            s = pair * 2 + a
            if k:
                seq_wait(5, mid_all, s)
            else:

                @pl.when(s != seq)
                def _():
                    seq_wait(5, mid_all, s)

            m = mid_all[s].astype(F32)
            squares = squares + m * m
            parts.append((m * gain2[pl.ds(s, 1), :]).astype(BF16))
        both = jnp.concatenate(parts, axis=1)
        rows = pl.ds(pl.multiple_of(pair * 256, 256), 256)
        gate = gate + dot(both, wg[rows, :])
        up = up + dot(both, wu[rows, :])
    inv_mlp = lax.rsqrt(jnp.sum(squares, axis=1, keepdims=True) / width + EPSILON)
    gate = gate * inv_mlp
    hidden = (gate / (1.0 + jnp.exp(-gate)) * (up * inv_mlp)).astype(BF16)
    for ks in ((6, 7, 2, 3), (4, 5, 1, 0)):
        columns = [wd[:, pl.ds(pl.multiple_of(near[k] * 256, 256), 256)] for k in ks]
        down = dot(hidden, jnp.concatenate(columns, axis=1)).astype(BF16)
        for n, k in enumerate(ks):
            for a in range(2):
                s = near[k] * 2 + a
                d_send[s] = down[:, n * 256 + a * 128 : n * 256 + (a + 1) * 128]
                if k:
                    seq_copy(6, d_send.at[s], d_recv.at[seq], s).start()
                else:

                    @pl.when(s != seq)
                    def _():
                        seq_copy(6, d_send.at[s], d_recv.at[seq], s).start()

    d_recv[seq] = d_send[seq]
    seq_wait_all(6, d_recv)
    result = mid.astype(F32)
    for s in range(n_seq):
        result = result + d_recv[s].astype(F32)
    out_ref[...] = result.astype(BF16).reshape(out_ref.shape)

    sent(0, x_recv, n_own - 1)
    sent(2, o_recv, n_own - 1)
    sent(3, x_rows, n_seq - 1)

    @pl.when(jnp.logical_not(holds_own))
    def _():
        sent(3, x_rows, 1)

    sent(4, q_all, n_seq - 1)
    sent(5, acc_recv, n_seq - 1)
    sent(6, st_recv, n_seq - 1)
    sent(7, at_all, n_seq - 1)
    sent(8, mid_all, n_seq - 1)
    sent(9, d_recv, n_seq - 1)


def solution(mesh):
    n_tok, n_seq, n_kv = mesh.shape["tok"], mesh.shape["seq"], mesh.shape["kv"]
    n_own = n_tok * n_kv
    lanes = np.arange(128) % 32
    freq = (ROPE_BASE ** (-(lanes * 2.0 / 64))).astype(np.float32).reshape(1, 128)

    def per_device(
        token_ids,
        request_order,
        cache_lengths,
        embed_table,
        attn_gain,
        proj_query,
        proj_kv,
        kv_cache,
        proj_out,
        mlp_gain,
        proj_gate,
        proj_up,
        proj_down,
    ):
        n_req, steps = token_ids.shape
        ctx = kv_cache.shape[1]
        rows = n_req * steps
        r_own, r_seq = rows // n_own, rows // n_seq
        width = proj_query.shape[0]
        smem = pl.BlockSpec(memory_space=pltpu.SMEM)
        vmem = pl.BlockSpec(memory_space=pltpu.VMEM)
        hbm = pl.BlockSpec(memory_space=pl.ANY)
        weights = [
            embed_table,
            proj_query,
            proj_kv.reshape(width, 128),
            kv_cache.reshape(n_req, ctx, 128),
            proj_out,
            proj_gate,
            proj_up,
            proj_down,
        ]
        scratch = [pltpu.VMEM(w.shape, w.dtype) for w in weights]
        scratch += [
            pltpu.VMEM((n_req // 2, ctx, 128), BF16),
            pltpu.VMEM((n_seq, 128), F32),
            pltpu.VMEM((rows, 128), jnp.int32),
            pltpu.VMEM((n_own, r_own, 128), BF16),
            pltpu.VMEM((n_own, r_own, 128), BF16),
            pltpu.VMEM((n_seq // n_own, r_seq, 128), BF16),
            pltpu.VMEM((n_seq, r_seq, 128), BF16),
            pltpu.VMEM((n_seq, 2 * r_seq, 128), BF16),
            pltpu.VMEM((ctx, 128), F32),
            pltpu.VMEM((ctx, 128), F32),
            pltpu.VMEM((128, ctx), BF16),
            pltpu.VMEM((128, ctx), BF16),
            pltpu.VMEM((n_seq, 2 * r_seq, 128), BF16),
            pltpu.VMEM((n_seq, 2 * r_seq, 128), BF16),
            pltpu.VMEM((n_req // 8, 2, 128), F32),
            pltpu.VMEM((n_seq, 2, 128), F32),
            pltpu.VMEM((128, 128), F32),
            pltpu.VMEM((n_seq, r_seq, 256), BF16),
            pltpu.VMEM((n_own, r_own, 128), BF16),
            pltpu.VMEM((n_own, r_own, 128), BF16),
            pltpu.VMEM((n_seq, r_own, 128), BF16),
            pltpu.VMEM((n_seq, r_own, 128), BF16),
            pltpu.VMEM((n_seq, r_own, 128), BF16),
            pltpu.SemaphoreType.DMA((16,)),
            pltpu.SemaphoreType.DMA((10,)),
            pltpu.SemaphoreType.DMA((3, n_own)),
            pltpu.SemaphoreType.DMA((7, n_seq)),
        ]
        return pl.pallas_call(
            functools.partial(layer_kernel, n_tok, n_seq, n_kv),
            out_shape=jax.ShapeDtypeStruct((n_req // n_own, steps, 128), BF16),
            in_specs=[smem, smem, smem, vmem, vmem, vmem] + [hbm] * len(weights),
            out_specs=vmem,
            scratch_shapes=scratch,
            compiler_params=pltpu.CompilerParams(
                collective_id=0, has_side_effects=True, vmem_limit_bytes=64 * 1000 * 1000
            ),
            name="layer",
        )(
            token_ids.T,
            request_order,
            cache_lengths,
            attn_gain.reshape(n_seq, 128),
            mlp_gain.reshape(n_seq, 128),
            jnp.asarray(freq),
            *weights,
        )

    placed = (
        P(),
        P(),
        P(),
        P(("tok", "kv"), "seq"),
        P(),
        P(None, ("tok", "kv")),
        P(None, ("tok", "kv"), None),
        P(None, "seq", ("tok", "kv"), None),
        P(("tok", "kv"), "seq"),
        P(),
        P(None, "seq"),
        P(None, "seq"),
        P("seq", None),
    )
    return jax.shard_map(
        per_device,
        mesh=mesh,
        in_specs=placed,
        out_specs=P(("tok", "kv"), None, "seq"),
        check_vma=False,
    )
```

```python
import functools

import jax
import jax.numpy as jnp
import numpy as np
from jax import lax
from jax.experimental import pallas as pl
from jax.experimental.pallas import tpu as pltpu
from jax.sharding import PartitionSpec as P

EPSILON = 1e-05
ROPE_BASE = 1000000.0
FLOOR_SCORE = -1e30
MESH = pl.DeviceIdType.MESH
F32 = jnp.float32
BF16 = jnp.bfloat16


def iota(shape, dim):
    return lax.broadcasted_iota(jnp.int32, shape, dim)


def dot_nt(a, b):
    return lax.dot_general(a, b, (((1,), (1,)), ((), ())), preferred_element_type=F32)


def dot(a, b):
    return jnp.dot(a, b, preferred_element_type=F32)


def interleave(tiles, count, size):
    return jnp.concatenate(
        [t[i * size : (i + 1) * size] for i in range(count) for t in tiles], axis=0
    )


def layer_kernel(
    n_tok,
    n_seq,
    n_kv,
    ids_hbm,
    order_hbm,
    len_hbm,
    gain_hbm,
    gain2_hbm,
    freq_hbm,
    table_hbm,
    wq_hbm,
    wkv_hbm,
    cache_hbm,
    wo_hbm,
    wg_hbm,
    wu_hbm,
    wd_hbm,
    out_ref,
    ids_ref,
    order_ref,
    len_ref,
    gain_ref,
    gain2_ref,
    freq_ref,
    table,
    wq,
    wkv,
    cache,
    wo,
    wg,
    wu,
    wd,
    keys,
    gain2,
    ids_v,
    x_send,
    x_recv,
    x_own_v,
    x_rows,
    q_all,
    s_even,
    s_odd,
    p_even,
    p_odd,
    acc_send,
    acc_recv,
    st_send,
    st_recv,
    st_t,
    at_all,
    o_send,
    o_recv,
    mid_all,
    d_send,
    d_recv,
    load_sem,
    send_sem,
    yc_sem,
    seq_sem,
):
    n_own = n_tok * n_kv
    tok = lax.axis_index("tok")
    seq = lax.axis_index("seq")
    kv = lax.axis_index("kv")
    own = tok * n_kv + kv
    vocab = table.shape[0]
    ctx = cache.shape[1]
    n_req = cache.shape[0]
    steps = 4
    n_rows = n_req * steps
    rows_own = n_rows // n_own
    rows_seq = n_rows // n_seq
    slots_seq = rows_seq // steps
    halves = n_seq // n_own
    width = n_seq * 128

    def seq_peer(s):
        return (tok, s, kv)

    def own_peer(g):
        return (g // n_kv, seq, lax.rem(g, n_kv))

    loads = []

    def load(src, dst):
        copy = pltpu.make_async_copy(src, dst, load_sem.at[len(loads)])
        copy.start()
        loads.append(copy)
        return copy

    table_load = load(table_hbm, table)
    small_loads = [load(ids_hbm, ids_ref), load(order_hbm, order_ref), load(len_hbm, len_ref)]
    barrier = pltpu.get_barrier_semaphore()
    for d in range(1, n_own):
        pl.semaphore_signal(
            barrier, inc=1, device_id=own_peer(lax.rem(own + d, n_own)), device_id_type=MESH
        )
    for d in range(1, n_seq):
        pl.semaphore_signal(
            barrier, inc=1, device_id=seq_peer(lax.rem(seq + d, n_seq)), device_id_type=MESH
        )
    gain_loads = [load(gain_hbm, gain_ref), load(gain2_hbm, gain2_ref), load(freq_hbm, freq_ref)]
    wq_load = load(wq_hbm, wq)
    wkv_load = load(wkv_hbm, wkv)
    chunk = 8
    cache_loads = [
        load(cache_hbm.at[pl.ds(c, chunk)], cache.at[pl.ds(c, chunk)])
        for c in range(0, n_req, chunk)
    ]
    wo_load = load(wo_hbm, wo)
    wg_load = load(wg_hbm, wg)
    wu_load = load(wu_hbm, wu)
    wd_load = load(wd_hbm, wd)

    def own_copy(phase, src, dst, g):
        return pltpu.make_async_remote_copy(
            src_ref=src,
            dst_ref=dst,
            send_sem=send_sem.at[phase],
            recv_sem=yc_sem.at[phase, own],
            device_id=own_peer(g),
            device_id_type=MESH,
        )

    def seq_copy(phase, src, dst, s):
        return pltpu.make_async_remote_copy(
            src_ref=src,
            dst_ref=dst,
            send_sem=send_sem.at[phase + 3],
            recv_sem=seq_sem.at[phase, seq],
            device_id=seq_peer(s),
            device_id_type=MESH,
        )

    owners = [
        lax.rem(tok + dt, n_tok) * n_kv + lax.rem(kv + dk, n_kv)
        for dt, dk in ((2, 0), (2, 1), (1, 0), (1, 1), (3, 0), (3, 1), (0, 1))
    ]

    def own_wait(phase, dst):
        for g in owners:
            pltpu.make_async_copy(dst.at[g], dst.at[g], yc_sem.at[phase, g]).wait()

    def seq_wait(phase, dst, s):
        pltpu.make_async_copy(dst.at[s], dst.at[s], seq_sem.at[phase, s]).wait()

    def seq_wait_all(phase, dst):
        for d in range(1, n_seq):
            seq_wait(phase, dst, lax.rem(seq + d, n_seq))

    def sent(index, buffer, count):
        part = buffer.at[pl.ds(0, count)]
        pltpu.make_async_copy(part, part, send_sem.at[index]).wait()

    def pair_at(k):
        dz = lax.rem(k + k // 4, 4)
        return lax.rem(seq // 4 + dz, n_seq // 4) * 2 + lax.rem(seq // 2 + k // 4, 2)

    near = [pair_at(jnp.int32(k)) for k in (0, 7, 1, 3, 4, 6, 2, 5)]
    far = (7, 6, 5, 4, 3, 2, 1, 0)

    sub8 = iota((8, 128), 0)

    def ids_block(b, carry):
        value = jnp.zeros((8, 128), jnp.int32)
        for i in range(8):
            request = order_ref[b * 2 + i // steps]
            value = jnp.where(sub8 == i, ids_ref[i % steps, request], value)
        ids_v[pl.ds(pl.multiple_of(b * 8, 8), 8), :] = value
        return carry

    for c in small_loads:
        c.wait()
    lax.fori_loop(0, n_rows // 8, ids_block, 0)

    table_load.wait()
    kt = 512
    wide_ids = jnp.concatenate([ids_v[...]] * (kt // 128), axis=1) - own * vocab
    lane_k = iota((n_rows, kt), 1)

    def pick(c, acc):
        hot = jnp.where(wide_ids == lane_k + c * kt, 1.0, 0.0).astype(BF16)
        return acc + dot(hot, table[pl.ds(pl.multiple_of(c * kt, kt), kt), :])

    picked = lax.fori_loop(0, vocab // kt, pick, jnp.zeros((n_rows, 128), F32)).astype(BF16)
    x_send[...] = picked.reshape(n_own, rows_own, 128)

    pl.semaphore_wait(barrier, n_own - 1 + n_seq - 1)

    for g in owners:
        own_copy(0, x_send.at[g], x_recv.at[own], g).start()
    x_recv[own] = x_send[own]
    own_wait(0, x_recv)
    x_own = x_recv[0].astype(F32)
    for g in range(1, n_own):
        x_own = x_own + x_recv[g].astype(F32)
    x_own_v[...] = x_own.astype(BF16).reshape(halves, rows_seq, 128)

    def x_copy(half, g):
        s = own * halves + half
        return pltpu.make_async_remote_copy(
            src_ref=x_own_v.at[half],
            dst_ref=x_rows.at[seq],
            send_sem=send_sem.at[3],
            recv_sem=seq_sem.at[0, seq],
            device_id=(g // n_kv, s, lax.rem(g, n_kv)),
            device_id_type=MESH,
        )

    holds_own = own == seq // halves
    for half in range(halves):
        for d in range(1, n_own):
            x_copy(half, lax.rem(own + d, n_own)).start()

        @pl.when(own * halves + half != seq)
        def _():
            x_copy(half, own).start()

    @pl.when(holds_own)
    def _():
        x_rows[seq] = x_own_v[lax.rem(seq, halves)]

    for c in cache_loads:
        c.wait()

    def pack(m, carry):
        size = 256
        low = iota((size, 128), 1) < 64
        for t in range(ctx // size):
            a = cache[order_ref[2 * m], t * size : (t + 1) * size, :]
            b = cache[order_ref[2 * m + 1], t * size : (t + 1) * size, :]
            keys[m, t * size : (t + 1) * size, :] = jnp.where(low, a, pltpu.roll(b, 64, 1))
        return carry

    lax.fori_loop(0, n_req // 2, pack, 0)

    for c in gain_loads:
        c.wait()
    gain2[...] = gain2_ref[...].astype(F32)

    row16 = iota((rows_seq, 128), 0)
    lane16 = iota((rows_seq, 128), 1)
    base_pos = jnp.zeros((rows_seq, 128), jnp.int32)
    for i in range(slots_seq):
        length = len_ref[order_ref[seq * slots_seq + i]]
        base_pos = jnp.where(row16 // steps == i, length, base_pos)
    position = (base_pos + lax.rem(row16, steps)).astype(F32)
    angle = position * freq_ref[...]
    turns = jnp.round(angle * (1.0 / (2.0 * np.pi)))
    angle = angle - turns * 6.28125
    angle = angle - turns * 0.0019350051879882812
    angle = angle - turns * 3.0199159819e-07
    cosine = jnp.cos(angle)
    sine = jnp.sin(angle)
    front = lax.rem(lane16, 64) < 32

    def rotate(v):
        swapped = jnp.where(front, -pltpu.roll(v, 96, 1), pltpu.roll(v, 32, 1))
        return v * cosine + swapped * sine

    gain = jnp.concatenate([gain_ref[s : s + 1, :].astype(F32) for s in range(n_seq)], axis=1)
    wq_load.wait()
    wkv_load.wait()

    for s in range(n_seq):

        @pl.when(jnp.logical_not(holds_own) | (seq != s))
        def _():
            seq_wait(0, x_rows, s)

    x16 = jnp.concatenate([x_rows[s] for s in range(n_seq)], axis=1).astype(F32)
    inv_attn = lax.rsqrt(jnp.sum(x16 * x16, axis=1, keepdims=True) / width + EPSILON)
    scaled = (x16 * gain).astype(BF16)
    q_raw = dot(scaled, wq[...]) * inv_attn
    kv_raw = dot(scaled, wkv[...]) * inv_attn
    q_tiles = [rotate(q_raw[:, t * 128 : (t + 1) * 128]) for t in range(2)]
    query = interleave(q_tiles, slots_seq, steps).astype(BF16)
    q_all[seq] = query
    for k in far:
        for a in range(2):
            s = near[k] * 2 + a
            if k:
                seq_copy(1, q_all.at[seq], q_all.at[seq], s).start()
            else:

                @pl.when(s != seq)
                def _():
                    seq_copy(1, q_all.at[seq], q_all.at[seq], s).start()

    rows_q = 2 * rows_seq
    low16 = lane16 < 64
    low32 = iota((rows_q, 128), 1) < 64
    fresh = jnp.where(low16, rotate(kv_raw), kv_raw).astype(BF16).astype(F32)
    key_lo = jnp.where(low16, fresh, 0.0)
    val_hi = jnp.where(low16, 0.0, fresh)
    f_keys = [key_lo.astype(BF16), pltpu.roll(key_lo, 64, 1).astype(BF16)]
    f_vals = [pltpu.roll(val_hi, 64, 1).astype(BF16), val_hi.astype(BF16)]
    r_i = iota((rows_q, rows_seq), 0)
    c_i = iota((rows_q, rows_seq), 1)
    causal = (r_i // (2 * steps) == c_i // steps) & (lax.rem(c_i, steps) <= lax.rem(r_i, steps))
    f_peak, f_mass, f_acc = [], [], []
    for hb in range(2):
        t = jnp.where(causal, dot_nt(query, f_keys[hb]) * 0.125, FLOOR_SCORE)
        peak = jnp.max(t, axis=1, keepdims=True)
        w = jnp.where(causal, jnp.exp(t - peak), 0.0).astype(BF16)
        f_peak.append(peak)
        f_mass.append(jnp.sum(w.astype(F32), axis=1, keepdims=True))
        f_acc.append(dot(w, f_vals[hb]))

    group = 8
    n_group = n_req // group
    pt = 512
    lane_slot = iota((1, 128), 1) // 16
    low8 = iota((8, 128), 1) < 64

    def arrive(k):
        for a in range(2):
            s = pair_at(k) * 2 + a

            @pl.when(s != seq)
            def _():
                seq_wait(1, q_all, s)

    def score(k, s_scr):
        grp = pair_at(k)
        q64 = q_all[pl.ds(grp * 2, 2)].reshape(2 * rows_q, 128).astype(F32) * 0.125
        r64 = pltpu.roll(q64, 64, 1)
        zero = jnp.zeros((32, 128), F32)
        columns = []
        for m in range(group // 2):
            e, o = slice(16 * m, 16 * m + 8), slice(16 * m + 8, 16 * m + 16)
            block = jnp.concatenate(
                [
                    jnp.where(low8, q64[e], 0.0),
                    jnp.where(low8, r64[e], 0.0),
                    jnp.where(low8, 0.0, r64[o]),
                    jnp.where(low8, 0.0, q64[o]),
                ],
                axis=0,
            )
            columns.append(
                jnp.concatenate([block if i == m else zero for i in range(group // 2)], axis=0)
            )
        rhs = jnp.concatenate(columns, axis=1).astype(BF16)
        lengths = jnp.zeros((1, 128), jnp.int32)
        for r in range(group):
            lengths = jnp.where(lane_slot == r, len_ref[order_ref[grp * group + r]], lengths)
        lengths = lengths - seq * ctx
        peak = jnp.full((1, 128), FLOOR_SCORE, F32)
        for t in range(ctx // pt):
            lhs = jnp.concatenate(
                [keys[grp * 4 + m, t * pt : (t + 1) * pt, :] for m in range(group // 2)], axis=1
            )
            live = iota((pt, 128), 0) + t * pt < lengths
            scores = jnp.where(live, dot_nt(lhs, rhs), FLOOR_SCORE)
            s_scr[t * pt : (t + 1) * pt, :] = scores
            peak = jnp.maximum(peak, jnp.max(scores, axis=0, keepdims=True))
        return peak, lengths

    def weigh(k, s_scr, p_scr, peak, lengths):
        grp = pair_at(k)
        shift = jnp.where(lengths > 0, peak, 0.0)
        mass = jnp.zeros((1, 128), F32)
        for t in range(ctx // pt):
            w = jnp.exp(s_scr[t * pt : (t + 1) * pt, :] - shift).astype(BF16)
            mass = mass + jnp.sum(w.astype(F32), axis=0, keepdims=True)
            p_scr[:, t * pt : (t + 1) * pt] = w.T
        st_send[grp] = jnp.concatenate([peak, mass], axis=0)
        for a in range(2):
            pieces = []
            for i in range(0, slots_seq, 2):
                r = a * slots_seq + i
                both = jnp.concatenate(
                    [cache[order_ref[grp * group + r + e]] for e in range(2)], axis=1
                )
                total = dot(p_scr[r * 16 : r * 16 + 32, :], both)
                for e in range(2):
                    tile = total[16 * e : 16 * e + 16, e * 128 : e * 128 + 128]
                    pieces.append(jnp.where(low8, pltpu.roll(tile[:8], 64, 1), tile[8:]))
            acc_send[grp * 2 + a] = jnp.concatenate(pieces, axis=0).astype(BF16)

    def deliver(k):
        grp = pair_at(k)
        for a in range(2):
            s = grp * 2 + a

            @pl.when(s != seq)
            def _():
                seq_copy(3, st_send.at[grp], st_recv.at[seq], s).start()
                seq_copy(2, acc_send.at[s], acc_recv.at[seq], s).start()

    def attend(i, carry):
        arrive(2 * i + 1)
        following = score(2 * i + 1, s_odd)
        weigh(2 * i, s_even, p_even, *carry)
        deliver(2 * i)
        arrive(2 * i + 2)
        carry = score(2 * i + 2, s_even)
        weigh(2 * i + 1, s_odd, p_odd, *following)
        deliver(2 * i + 1)
        return carry

    arrive(jnp.int32(0))
    carry = lax.fori_loop(0, n_group // 2 - 1, attend, score(jnp.int32(0), s_even))
    last = jnp.int32(n_group - 2)
    arrive(last + 1)
    following = score(last + 1, s_odd)
    weigh(last, s_even, p_even, *carry)
    deliver(last)
    weigh(last + 1, s_odd, p_odd, *following)
    deliver(last + 1)

    acc_recv[seq] = acc_send[seq]
    st_recv[seq] = st_send[seq // 2]
    seq_wait_all(3, st_recv)
    stats = jnp.concatenate([st_recv[:, 0, :], st_recv[:, 1, :]], axis=0)
    st_t[...] = jnp.concatenate([stats, jnp.zeros((128 - 2 * n_seq, 128), F32)], axis=0).T
    mine = st_t[pl.ds(pl.multiple_of(lax.rem(seq, 2) * 64, 64), 64), :]
    shares, f_share = [], []
    for hb in range(2):
        block = jnp.concatenate(
            [mine[16 * i + 8 * hb : 16 * i + 8 * hb + 8] for i in range(slots_seq)], axis=0
        )
        peaks, masses = block[:, :n_seq], block[:, n_seq : 2 * n_seq]
        top = jnp.maximum(jnp.max(peaks, axis=1, keepdims=True), f_peak[hb])
        factor = jnp.exp(peaks - top)
        f_factor = jnp.exp(f_peak[hb] - top)
        denom = jnp.sum(factor * masses, axis=1, keepdims=True) + f_factor * f_mass[hb]
        shares.append(factor / denom)
        f_share.append(f_factor / denom)
    weights = [jnp.where(low32, shares[0][:, s : s + 1], shares[1][:, s : s + 1]) for s in range(n_seq)]
    attended = f_acc[0] * f_share[0] + f_acc[1] * f_share[1]
    seq_wait_all(2, acc_recv)
    for s in range(n_seq):
        attended = attended + weights[s] * acc_recv[s].astype(F32)

    at_rows = [
        jnp.concatenate(
            [attended[8 * i + 4 * t : 8 * i + 4 * t + 4] for i in range(slots_seq)], axis=0
        )
        for t in range(2)
    ]
    at_all[seq] = jnp.concatenate(at_rows, axis=1).astype(BF16)
    for k in far:
        for a in range(2):
            s = near[k] * 2 + a
            if k:
                seq_copy(4, at_all.at[seq], at_all.at[seq], s).start()
            else:

                @pl.when(s != seq)
                def _():
                    seq_copy(4, at_all.at[seq], at_all.at[seq], s).start()
    wo_load.wait()
    seq_wait_all(4, at_all)
    partial = dot(at_all[...].reshape(n_rows, 256), wo[...]).astype(BF16)
    o_send[...] = partial.reshape(n_own, rows_own, 128)
    for g in owners:
        own_copy(2, o_send.at[g], o_recv.at[own], g).start()
    o_recv[own] = o_send[own]
    own_wait(2, o_recv)
    attn = o_recv[0].astype(F32)
    for g in range(1, n_own):
        attn = attn + o_recv[g].astype(F32)
    mid = (x_own + attn).astype(BF16)
    mid_all[seq] = mid
    for k in far:
        for a in range(2):
            s = near[k] * 2 + a
            if k:
                seq_copy(5, mid_all.at[seq], mid_all.at[seq], s).start()
            else:

                @pl.when(s != seq)
                def _():
                    seq_copy(5, mid_all.at[seq], mid_all.at[seq], s).start()

    wg_load.wait()
    wu_load.wait()
    wd_load.wait()
    ff = wg.shape[1]
    gate = jnp.zeros((rows_own, ff), F32)
    up = jnp.zeros((rows_own, ff), F32)
    squares = jnp.zeros((rows_own, 128), F32)
    for k in range(n_seq // 2):
        pair = near[k]
        parts = []
        for a in range(2):
            s = pair * 2 + a
            if k:
                seq_wait(5, mid_all, s)
            else:

                @pl.when(s != seq)
                def _():
                    seq_wait(5, mid_all, s)

            m = mid_all[s].astype(F32)
            squares = squares + m * m
            parts.append((m * gain2[pl.ds(s, 1), :]).astype(BF16))
        both = jnp.concatenate(parts, axis=1)
        rows = pl.ds(pl.multiple_of(pair * 256, 256), 256)
        gate = gate + dot(both, wg[rows, :])
        up = up + dot(both, wu[rows, :])
    inv_mlp = lax.rsqrt(jnp.sum(squares, axis=1, keepdims=True) / width + EPSILON)
    gate = gate * inv_mlp
    hidden = (gate / (1.0 + jnp.exp(-gate)) * (up * inv_mlp)).astype(BF16)
    for ks in (far[:4], far[4:]):
        columns = [wd[:, pl.ds(pl.multiple_of(near[k] * 256, 256), 256)] for k in ks]
        down = dot(hidden, jnp.concatenate(columns, axis=1)).astype(BF16)
        for n, k in enumerate(ks):
            for a in range(2):
                s = near[k] * 2 + a
                d_send[s] = down[:, n * 256 + a * 128 : n * 256 + (a + 1) * 128]
                if k:
                    seq_copy(6, d_send.at[s], d_recv.at[seq], s).start()
                else:

                    @pl.when(s != seq)
                    def _():
                        seq_copy(6, d_send.at[s], d_recv.at[seq], s).start()

    d_recv[seq] = d_send[seq]
    seq_wait_all(6, d_recv)
    result = mid.astype(F32)
    for s in range(n_seq):
        result = result + d_recv[s].astype(F32)
    out_ref[...] = result.astype(BF16).reshape(out_ref.shape)

    sent(0, x_recv, n_own - 1)
    sent(2, o_recv, n_own - 1)
    sent(3, x_rows, n_seq - 1)

    @pl.when(jnp.logical_not(holds_own))
    def _():
        sent(3, x_rows, 1)

    sent(4, q_all, n_seq - 1)
    sent(5, acc_recv, n_seq - 1)
    sent(6, st_recv, n_seq - 1)
    sent(7, at_all, n_seq - 1)
    sent(8, mid_all, n_seq - 1)
    sent(9, d_recv, n_seq - 1)


def solution(mesh):
    n_tok, n_seq, n_kv = mesh.shape["tok"], mesh.shape["seq"], mesh.shape["kv"]
    n_own = n_tok * n_kv
    lanes = np.arange(128) % 32
    freq = (ROPE_BASE ** (-(lanes * 2.0 / 64))).astype(np.float32).reshape(1, 128)

    def per_device(
        token_ids,
        request_order,
        cache_lengths,
        embed_table,
        attn_gain,
        proj_query,
        proj_kv,
        kv_cache,
        proj_out,
        mlp_gain,
        proj_gate,
        proj_up,
        proj_down,
    ):
        n_req, steps = token_ids.shape
        ctx = kv_cache.shape[1]
        rows = n_req * steps
        r_own, r_seq = rows // n_own, rows // n_seq
        width = proj_query.shape[0]
        vmem = pl.BlockSpec(memory_space=pltpu.VMEM)
        hbm = pl.BlockSpec(memory_space=pl.ANY)
        weights = [
            embed_table,
            proj_query,
            proj_kv.reshape(width, 128),
            kv_cache.reshape(n_req, ctx, 128),
            proj_out,
            proj_gate,
            proj_up,
            proj_down,
        ]
        scratch = [
            pltpu.SMEM((steps, n_req), jnp.int32),
            pltpu.SMEM((n_req,), jnp.int32),
            pltpu.SMEM((n_req,), jnp.int32),
            pltpu.VMEM((n_seq, 128), BF16),
            pltpu.VMEM((n_seq, 128), BF16),
            pltpu.VMEM((1, 128), F32),
        ]
        scratch += [pltpu.VMEM(w.shape, w.dtype) for w in weights]
        scratch += [
            pltpu.VMEM((n_req // 2, ctx, 128), BF16),
            pltpu.VMEM((n_seq, 128), F32),
            pltpu.VMEM((rows, 128), jnp.int32),
            pltpu.VMEM((n_own, r_own, 128), BF16),
            pltpu.VMEM((n_own, r_own, 128), BF16),
            pltpu.VMEM((n_seq // n_own, r_seq, 128), BF16),
            pltpu.VMEM((n_seq, r_seq, 128), BF16),
            pltpu.VMEM((n_seq, 2 * r_seq, 128), BF16),
            pltpu.VMEM((ctx, 128), F32),
            pltpu.VMEM((ctx, 128), F32),
            pltpu.VMEM((128, ctx), BF16),
            pltpu.VMEM((128, ctx), BF16),
            pltpu.VMEM((n_seq, 2 * r_seq, 128), BF16),
            pltpu.VMEM((n_seq, 2 * r_seq, 128), BF16),
            pltpu.VMEM((n_req // 8, 2, 128), F32),
            pltpu.VMEM((n_seq, 2, 128), F32),
            pltpu.VMEM((128, 128), F32),
            pltpu.VMEM((n_seq, r_seq, 256), BF16),
            pltpu.VMEM((n_own, r_own, 128), BF16),
            pltpu.VMEM((n_own, r_own, 128), BF16),
            pltpu.VMEM((n_seq, r_own, 128), BF16),
            pltpu.VMEM((n_seq, r_own, 128), BF16),
            pltpu.VMEM((n_seq, r_own, 128), BF16),
            pltpu.SemaphoreType.DMA((21,)),
            pltpu.SemaphoreType.DMA((10,)),
            pltpu.SemaphoreType.DMA((3, n_own)),
            pltpu.SemaphoreType.DMA((7, n_seq)),
        ]
        return pl.pallas_call(
            functools.partial(layer_kernel, n_tok, n_seq, n_kv),
            out_shape=jax.ShapeDtypeStruct((n_req // n_own, steps, 128), BF16),
            in_specs=[hbm] * (6 + len(weights)),
            out_specs=vmem,
            scratch_shapes=scratch,
            compiler_params=pltpu.CompilerParams(
                collective_id=0, has_side_effects=True, vmem_limit_bytes=64 * 1000 * 1000
            ),
            name="layer",
        )(
            token_ids.T,
            request_order,
            cache_lengths,
            attn_gain.reshape(n_seq, 128),
            mlp_gain.reshape(n_seq, 128),
            jnp.asarray(freq),
            *weights,
        )

    placed = (
        P(),
        P(),
        P(),
        P(("tok", "kv"), "seq"),
        P(),
        P(None, ("tok", "kv")),
        P(None, ("tok", "kv"), None),
        P(None, "seq", ("tok", "kv"), None),
        P(("tok", "kv"), "seq"),
        P(),
        P(None, "seq"),
        P(None, "seq"),
        P("seq", None),
    )
    return jax.shard_map(
        per_device,
        mesh=mesh,
        in_specs=placed,
        out_specs=P(("tok", "kv"), None, "seq"),
        check_vma=False,
    )
```

```python
import functools

import jax
import jax.numpy as jnp
import numpy as np
from jax import lax
from jax.experimental import pallas as pl
from jax.experimental.pallas import tpu as pltpu
from jax.sharding import PartitionSpec as P

EPSILON = 1e-05
ROPE_BASE = 1000000.0
FLOOR_SCORE = -1e30
MESH = pl.DeviceIdType.MESH
F32 = jnp.float32
BF16 = jnp.bfloat16


def iota(shape, dim):
    return lax.broadcasted_iota(jnp.int32, shape, dim)


def dot_nt(a, b):
    return lax.dot_general(a, b, (((1,), (1,)), ((), ())), preferred_element_type=F32)


def dot(a, b):
    return jnp.dot(a, b, preferred_element_type=F32)


def interleave(tiles, count, size):
    return jnp.concatenate(
        [t[i * size : (i + 1) * size] for i in range(count) for t in tiles], axis=0
    )


def layer_kernel(
    n_tok,
    n_seq,
    n_kv,
    ids_hbm,
    order_hbm,
    len_hbm,
    gain_hbm,
    gain2_hbm,
    freq_hbm,
    table_hbm,
    wq_hbm,
    wkv_hbm,
    cache_hbm,
    wo_hbm,
    wg_hbm,
    wu_hbm,
    wd_hbm,
    out_ref,
    ids_ref,
    order_ref,
    len_ref,
    gain_ref,
    gain2_ref,
    freq_ref,
    table,
    wq,
    wkv,
    cache,
    wo,
    wg,
    wu,
    wd,
    keys,
    gain2,
    ids_v,
    x_send,
    x_recv,
    x_own_v,
    x_rows,
    q_all,
    s_even,
    s_odd,
    p_even,
    p_odd,
    acc_send,
    acc_recv,
    st_send,
    st_recv,
    st_t,
    o_send,
    o_recv,
    mid_all,
    d_send,
    d_recv,
    load_sem,
    send_sem,
    yc_sem,
    seq_sem,
):
    n_own = n_tok * n_kv
    tok = lax.axis_index("tok")
    seq = lax.axis_index("seq")
    kv = lax.axis_index("kv")
    own = tok * n_kv + kv
    vocab = table.shape[0]
    ctx = cache.shape[1]
    n_req = cache.shape[0]
    steps = 4
    n_rows = n_req * steps
    rows_own = n_rows // n_own
    rows_seq = n_rows // n_seq
    slots_seq = rows_seq // steps
    halves = n_seq // n_own
    width = n_seq * 128

    def seq_peer(s):
        return (tok, s, kv)

    def own_peer(g):
        return (g // n_kv, seq, lax.rem(g, n_kv))

    loads = []

    def load(src, dst):
        copy = pltpu.make_async_copy(src, dst, load_sem.at[len(loads)])
        copy.start()
        loads.append(copy)
        return copy

    table_load = load(table_hbm, table)
    small_loads = [load(ids_hbm, ids_ref), load(order_hbm, order_ref), load(len_hbm, len_ref)]
    wo_load = load(wo_hbm, wo.at[seq])
    barrier = pltpu.get_barrier_semaphore()
    for d in range(1, n_own):
        pl.semaphore_signal(
            barrier, inc=1, device_id=own_peer(lax.rem(own + d, n_own)), device_id_type=MESH
        )
    for d in range(1, n_seq):
        pl.semaphore_signal(
            barrier, inc=1, device_id=seq_peer(lax.rem(seq + d, n_seq)), device_id_type=MESH
        )
    gain_loads = [load(gain_hbm, gain_ref), load(gain2_hbm, gain2_ref), load(freq_hbm, freq_ref)]
    wq_load = load(wq_hbm, wq)
    wkv_load = load(wkv_hbm, wkv)
    chunk = 8
    cache_loads = [
        load(cache_hbm.at[pl.ds(c, chunk)], cache.at[pl.ds(c, chunk)])
        for c in range(0, n_req, chunk)
    ]
    wg_load = load(wg_hbm, wg)
    wu_load = load(wu_hbm, wu)
    wd_load = load(wd_hbm, wd)

    def own_copy(phase, src, dst, g):
        return pltpu.make_async_remote_copy(
            src_ref=src,
            dst_ref=dst,
            send_sem=send_sem.at[phase],
            recv_sem=yc_sem.at[phase, own],
            device_id=own_peer(g),
            device_id_type=MESH,
        )

    def seq_copy(phase, src, dst, s):
        return pltpu.make_async_remote_copy(
            src_ref=src,
            dst_ref=dst,
            send_sem=send_sem.at[phase + 3],
            recv_sem=seq_sem.at[phase, seq],
            device_id=seq_peer(s),
            device_id_type=MESH,
        )

    owners = [
        lax.rem(tok + dt, n_tok) * n_kv + lax.rem(kv + dk, n_kv)
        for dt, dk in ((2, 0), (2, 1), (1, 0), (1, 1), (3, 0), (3, 1), (0, 1))
    ]

    def own_wait(phase, dst):
        for g in owners:
            pltpu.make_async_copy(dst.at[g], dst.at[g], yc_sem.at[phase, g]).wait()

    def seq_wait(phase, dst, s):
        pltpu.make_async_copy(dst.at[s], dst.at[s], seq_sem.at[phase, s]).wait()

    def seq_wait_all(phase, dst):
        for d in range(1, n_seq):
            seq_wait(phase, dst, lax.rem(seq + d, n_seq))

    def sent(index, buffer, count):
        part = buffer.at[pl.ds(0, count)]
        pltpu.make_async_copy(part, part, send_sem.at[index]).wait()

    def pair_at(k):
        dz = lax.rem(k + k // 4, 4)
        return lax.rem(seq // 4 + dz, n_seq // 4) * 2 + lax.rem(seq // 2 + k // 4, 2)

    near = [pair_at(jnp.int32(k)) for k in (0, 7, 1, 3, 4, 6, 2, 5)]
    far = (7, 6, 5, 4, 3, 2, 1, 0)

    sub8 = iota((8, 128), 0)

    def ids_block(b, carry):
        value = jnp.zeros((8, 128), jnp.int32)
        for i in range(8):
            request = order_ref[b * 2 + i // steps]
            value = jnp.where(sub8 == i, ids_ref[i % steps, request], value)
        ids_v[pl.ds(pl.multiple_of(b * 8, 8), 8), :] = value
        return carry

    for c in small_loads:
        c.wait()
    lax.fori_loop(0, n_rows // 8, ids_block, 0)

    table_load.wait()
    kt = 512
    wide_ids = jnp.concatenate([ids_v[...]] * (kt // 128), axis=1) - own * vocab
    lane_k = iota((n_rows, kt), 1)

    def pick(c, acc):
        hot = jnp.where(wide_ids == lane_k + c * kt, 1.0, 0.0).astype(BF16)
        return acc + dot(hot, table[pl.ds(pl.multiple_of(c * kt, kt), kt), :])

    picked = lax.fori_loop(0, vocab // kt, pick, jnp.zeros((n_rows, 128), F32)).astype(BF16)
    x_send[...] = picked.reshape(n_own, rows_own, 128)

    pl.semaphore_wait(barrier, n_own - 1 + n_seq - 1)

    for g in owners:
        own_copy(0, x_send.at[g], x_recv.at[own], g).start()

    def share_wo(k):
        for a in range(2):
            s = pair_at(k) * 2 + a

            @pl.when(s != seq)
            def _():
                seq_copy(7, wo.at[seq], wo.at[seq], s).start()

    wo_load.wait()
    share_wo(jnp.int32(2))
    share_wo(jnp.int32(5))
    x_recv[own] = x_send[own]
    own_wait(0, x_recv)
    x_own = x_recv[0].astype(F32)
    for g in range(1, n_own):
        x_own = x_own + x_recv[g].astype(F32)
    x_own_v[...] = x_own.astype(BF16).reshape(halves, rows_seq, 128)

    def x_copy(half, g):
        s = own * halves + half
        return pltpu.make_async_remote_copy(
            src_ref=x_own_v.at[half],
            dst_ref=x_rows.at[seq],
            send_sem=send_sem.at[3],
            recv_sem=seq_sem.at[0, seq],
            device_id=(g // n_kv, s, lax.rem(g, n_kv)),
            device_id_type=MESH,
        )

    holds_own = own == seq // halves
    for half in range(halves):
        for d in range(1, n_own):
            x_copy(half, lax.rem(own + d, n_own)).start()

        @pl.when(own * halves + half != seq)
        def _():
            x_copy(half, own).start()

    @pl.when(holds_own)
    def _():
        x_rows[seq] = x_own_v[lax.rem(seq, halves)]

    for c in cache_loads:
        c.wait()

    def pack(m, carry):
        size = 256
        low = iota((size, 128), 1) < 64
        for t in range(ctx // size):
            a = cache[order_ref[2 * m], t * size : (t + 1) * size, :]
            b = cache[order_ref[2 * m + 1], t * size : (t + 1) * size, :]
            keys[m, t * size : (t + 1) * size, :] = jnp.where(low, a, pltpu.roll(b, 64, 1))
        return carry

    lax.fori_loop(0, n_req // 2, pack, 0)

    for c in gain_loads:
        c.wait()
    gain2[...] = gain2_ref[...].astype(F32)

    row16 = iota((rows_seq, 128), 0)
    lane16 = iota((rows_seq, 128), 1)
    base_pos = jnp.zeros((rows_seq, 128), jnp.int32)
    for i in range(slots_seq):
        length = len_ref[order_ref[seq * slots_seq + i]]
        base_pos = jnp.where(row16 // steps == i, length, base_pos)
    position = (base_pos + lax.rem(row16, steps)).astype(F32)
    angle = position * freq_ref[...]
    turns = jnp.round(angle * (1.0 / (2.0 * np.pi)))
    angle = angle - turns * 6.28125
    angle = angle - turns * 0.0019350051879882812
    angle = angle - turns * 3.0199159819e-07
    cosine = jnp.cos(angle)
    sine = jnp.sin(angle)
    front = lax.rem(lane16, 64) < 32

    def rotate(v):
        swapped = jnp.where(front, -pltpu.roll(v, 96, 1), pltpu.roll(v, 32, 1))
        return v * cosine + swapped * sine

    gain = jnp.concatenate([gain_ref[s : s + 1, :].astype(F32) for s in range(n_seq)], axis=1)
    wq_load.wait()
    wkv_load.wait()

    for s in range(n_seq):

        @pl.when(jnp.logical_not(holds_own) | (seq != s))
        def _():
            seq_wait(0, x_rows, s)

    x16 = jnp.concatenate([x_rows[s] for s in range(n_seq)], axis=1).astype(F32)
    inv_attn = lax.rsqrt(jnp.sum(x16 * x16, axis=1, keepdims=True) / width + EPSILON)
    scaled = (x16 * gain).astype(BF16)
    q_raw = dot(scaled, wq[...]) * inv_attn
    kv_raw = dot(scaled, wkv[...]) * inv_attn
    q_tiles = [rotate(q_raw[:, t * 128 : (t + 1) * 128]) for t in range(2)]
    query = interleave(q_tiles, slots_seq, steps).astype(BF16)
    q_all[seq] = query
    for k in far:
        for a in range(2):
            s = near[k] * 2 + a
            if k:
                seq_copy(1, q_all.at[seq], q_all.at[seq], s).start()
            else:

                @pl.when(s != seq)
                def _():
                    seq_copy(1, q_all.at[seq], q_all.at[seq], s).start()

    rows_q = 2 * rows_seq
    low16 = lane16 < 64
    low32 = iota((rows_q, 128), 1) < 64
    fresh = jnp.where(low16, rotate(kv_raw), kv_raw).astype(BF16).astype(F32)
    key_lo = jnp.where(low16, fresh, 0.0)
    val_hi = jnp.where(low16, 0.0, fresh)
    f_keys = [key_lo.astype(BF16), pltpu.roll(key_lo, 64, 1).astype(BF16)]
    f_vals = [pltpu.roll(val_hi, 64, 1).astype(BF16), val_hi.astype(BF16)]
    r_i = iota((rows_q, rows_seq), 0)
    c_i = iota((rows_q, rows_seq), 1)
    causal = (r_i // (2 * steps) == c_i // steps) & (lax.rem(c_i, steps) <= lax.rem(r_i, steps))
    f_peak, f_mass, f_acc = [], [], []
    for hb in range(2):
        t = jnp.where(causal, dot_nt(query, f_keys[hb]) * 0.125, FLOOR_SCORE)
        peak = jnp.max(t, axis=1, keepdims=True)
        w = jnp.where(causal, jnp.exp(t - peak), 0.0).astype(BF16)
        f_peak.append(peak)
        f_mass.append(jnp.sum(w.astype(F32), axis=1, keepdims=True))
        f_acc.append(dot(w, f_vals[hb]))

    group = 8
    n_group = n_req // group
    pt = 512
    lane_slot = iota((1, 128), 1) // 16
    low8 = iota((8, 128), 1) < 64

    def arrive(k):
        for a in range(2):
            s = pair_at(k) * 2 + a

            @pl.when(s != seq)
            def _():
                seq_wait(1, q_all, s)

    def score(k, s_scr):
        grp = pair_at(k)
        q64 = q_all[pl.ds(grp * 2, 2)].reshape(2 * rows_q, 128).astype(F32) * 0.125
        r64 = pltpu.roll(q64, 64, 1)
        zero = jnp.zeros((32, 128), F32)
        columns = []
        for m in range(group // 2):
            e, o = slice(16 * m, 16 * m + 8), slice(16 * m + 8, 16 * m + 16)
            block = jnp.concatenate(
                [
                    jnp.where(low8, q64[e], 0.0),
                    jnp.where(low8, r64[e], 0.0),
                    jnp.where(low8, 0.0, r64[o]),
                    jnp.where(low8, 0.0, q64[o]),
                ],
                axis=0,
            )
            columns.append(
                jnp.concatenate([block if i == m else zero for i in range(group // 2)], axis=0)
            )
        rhs = jnp.concatenate(columns, axis=1).astype(BF16)
        lengths = jnp.zeros((1, 128), jnp.int32)
        for r in range(group):
            lengths = jnp.where(lane_slot == r, len_ref[order_ref[grp * group + r]], lengths)
        lengths = lengths - seq * ctx
        peak = jnp.full((1, 128), FLOOR_SCORE, F32)
        for t in range(ctx // pt):
            lhs = jnp.concatenate(
                [keys[grp * 4 + m, t * pt : (t + 1) * pt, :] for m in range(group // 2)], axis=1
            )
            live = iota((pt, 128), 0) + t * pt < lengths
            scores = jnp.where(live, dot_nt(lhs, rhs), FLOOR_SCORE)
            s_scr[t * pt : (t + 1) * pt, :] = scores
            peak = jnp.maximum(peak, jnp.max(scores, axis=0, keepdims=True))
        return peak, lengths

    def weigh(k, s_scr, p_scr, peak, lengths):
        grp = pair_at(k)
        shift = jnp.where(lengths > 0, peak, 0.0)
        mass = jnp.zeros((1, 128), F32)
        for t in range(ctx // pt):
            w = jnp.exp(s_scr[t * pt : (t + 1) * pt, :] - shift).astype(BF16)
            mass = mass + jnp.sum(w.astype(F32), axis=0, keepdims=True)
            p_scr[:, t * pt : (t + 1) * pt] = w.T
        st_send[grp] = jnp.concatenate([peak, mass], axis=0)
        for a in range(2):
            pieces = []
            for i in range(0, slots_seq, 2):
                r = a * slots_seq + i
                both = jnp.concatenate(
                    [cache[order_ref[grp * group + r + e]] for e in range(2)], axis=1
                )
                total = dot(p_scr[r * 16 : r * 16 + 32, :], both)
                for e in range(2):
                    tile = total[16 * e : 16 * e + 16, e * 128 : e * 128 + 128]
                    pieces.append(jnp.where(low8, pltpu.roll(tile[:8], 64, 1), tile[8:]))
            acc_send[grp * 2 + a] = jnp.concatenate(pieces, axis=0).astype(BF16)

    def deliver(k):
        grp = pair_at(k)
        for a in range(2):
            s = grp * 2 + a

            @pl.when(s != seq)
            def _():
                seq_copy(3, st_send.at[grp], st_recv.at[seq], s).start()
                seq_copy(2, acc_send.at[s], acc_recv.at[seq], s).start()

    def attend(i, carry):
        arrive(2 * i + 1)
        share_wo(4 + i + (i + 1) // 2)
        following = score(2 * i + 1, s_odd)
        weigh(2 * i, s_even, p_even, *carry)
        deliver(2 * i)
        arrive(2 * i + 2)
        share_wo(i + i // 2)
        carry = score(2 * i + 2, s_even)
        weigh(2 * i + 1, s_odd, p_odd, *following)
        deliver(2 * i + 1)
        return carry

    arrive(jnp.int32(0))
    carry = lax.fori_loop(0, n_group // 2 - 1, attend, score(jnp.int32(0), s_even))
    last = jnp.int32(n_group - 2)
    arrive(last + 1)
    following = score(last + 1, s_odd)
    weigh(last, s_even, p_even, *carry)
    deliver(last)
    weigh(last + 1, s_odd, p_odd, *following)
    deliver(last + 1)

    acc_recv[seq] = acc_send[seq]
    st_recv[seq] = st_send[seq // 2]
    seq_wait_all(3, st_recv)
    stats = jnp.concatenate([st_recv[:, 0, :], st_recv[:, 1, :]], axis=0)
    st_t[...] = jnp.concatenate([stats, jnp.zeros((128 - 2 * n_seq, 128), F32)], axis=0).T
    mine = st_t[pl.ds(pl.multiple_of(lax.rem(seq, 2) * 64, 64), 64), :]
    shares, f_share = [], []
    for hb in range(2):
        block = jnp.concatenate(
            [mine[16 * i + 8 * hb : 16 * i + 8 * hb + 8] for i in range(slots_seq)], axis=0
        )
        peaks, masses = block[:, :n_seq], block[:, n_seq : 2 * n_seq]
        top = jnp.maximum(jnp.max(peaks, axis=1, keepdims=True), f_peak[hb])
        factor = jnp.exp(peaks - top)
        f_factor = jnp.exp(f_peak[hb] - top)
        denom = jnp.sum(factor * masses, axis=1, keepdims=True) + f_factor * f_mass[hb]
        shares.append(factor / denom)
        f_share.append(f_factor / denom)
    weights = [jnp.where(low32, shares[0][:, s : s + 1], shares[1][:, s : s + 1]) for s in range(n_seq)]
    attended = f_acc[0] * f_share[0] + f_acc[1] * f_share[1]
    seq_wait_all(2, acc_recv)
    for s in range(n_seq):
        attended = attended + weights[s] * acc_recv[s].astype(F32)

    at_rows = [
        jnp.concatenate(
            [attended[8 * i + 4 * t : 8 * i + 4 * t + 4] for i in range(slots_seq)], axis=0
        )
        for t in range(2)
    ]
    at = jnp.concatenate(at_rows, axis=1).astype(BF16)
    holder = seq // halves
    slot = own * halves + lax.rem(seq, halves)

    def o_copy(s):
        return pltpu.make_async_remote_copy(
            src_ref=o_send.at[s],
            dst_ref=o_recv.at[slot],
            send_sem=send_sem.at[7],
            recv_sem=seq_sem.at[4, slot],
            device_id=(holder // n_kv, s, lax.rem(holder, n_kv)),
            device_id_type=MESH,
        )

    seq_wait_all(7, wo)
    for ks in (far[:4], far[4:]):
        columns = [wo[near[k] * 2 + a] for k in ks for a in range(2)]
        partial = dot(at, jnp.concatenate(columns, axis=1)).astype(BF16)
        for n, k in enumerate(ks):
            for a in range(2):
                s = near[k] * 2 + a
                o_send[s] = partial[:, n * 256 + a * 128 : n * 256 + (a + 1) * 128]
                if k:
                    o_copy(s).start()
                else:

                    @pl.when(jnp.logical_not(holds_own) | (s != seq))
                    def _():
                        o_copy(s).start()

    @pl.when(holds_own)
    def _():
        o_recv[seq] = o_send[seq]

    for s in range(n_seq):

        @pl.when(jnp.logical_not(holds_own) | (seq != s))
        def _():
            seq_wait(4, o_recv, s)

    attn_rows = []
    for half in range(halves):
        total = o_recv[half].astype(F32)
        for g in range(1, n_own):
            total = total + o_recv[g * halves + half].astype(F32)
        attn_rows.append(total)
    attn = jnp.concatenate(attn_rows, axis=0)
    mid = (x_own + attn).astype(BF16)
    mid_all[seq] = mid
    for k in far:
        for a in range(2):
            s = near[k] * 2 + a
            if k:
                seq_copy(5, mid_all.at[seq], mid_all.at[seq], s).start()
            else:

                @pl.when(s != seq)
                def _():
                    seq_copy(5, mid_all.at[seq], mid_all.at[seq], s).start()

    wg_load.wait()
    wu_load.wait()
    wd_load.wait()
    ff = wg.shape[1]
    gate = jnp.zeros((rows_own, ff), F32)
    up = jnp.zeros((rows_own, ff), F32)
    squares = jnp.zeros((rows_own, 128), F32)
    for k in range(n_seq // 2):
        pair = near[k]
        parts = []
        for a in range(2):
            s = pair * 2 + a
            if k:
                seq_wait(5, mid_all, s)
            else:

                @pl.when(s != seq)
                def _():
                    seq_wait(5, mid_all, s)

            m = mid_all[s].astype(F32)
            squares = squares + m * m
            parts.append((m * gain2[pl.ds(s, 1), :]).astype(BF16))
        both = jnp.concatenate(parts, axis=1)
        rows = pl.ds(pl.multiple_of(pair * 256, 256), 256)
        gate = gate + dot(both, wg[rows, :])
        up = up + dot(both, wu[rows, :])
    inv_mlp = lax.rsqrt(jnp.sum(squares, axis=1, keepdims=True) / width + EPSILON)
    gate = gate * inv_mlp
    hidden = (gate / (1.0 + jnp.exp(-gate)) * (up * inv_mlp)).astype(BF16)
    for ks in (far[:4], far[4:]):
        columns = [wd[:, pl.ds(pl.multiple_of(near[k] * 256, 256), 256)] for k in ks]
        down = dot(hidden, jnp.concatenate(columns, axis=1)).astype(BF16)
        for n, k in enumerate(ks):
            for a in range(2):
                s = near[k] * 2 + a
                d_send[s] = down[:, n * 256 + a * 128 : n * 256 + (a + 1) * 128]
                if k:
                    seq_copy(6, d_send.at[s], d_recv.at[seq], s).start()
                else:

                    @pl.when(s != seq)
                    def _():
                        seq_copy(6, d_send.at[s], d_recv.at[seq], s).start()

    d_recv[seq] = d_send[seq]
    seq_wait_all(6, d_recv)
    result = mid.astype(F32)
    for s in range(n_seq):
        result = result + d_recv[s].astype(F32)
    out_ref[...] = result.astype(BF16).reshape(out_ref.shape)

    sent(0, x_recv, n_own - 1)
    sent(3, x_rows, n_seq - 1)

    @pl.when(jnp.logical_not(holds_own))
    def _():
        sent(3, x_rows, 1)
        sent(7, o_recv, 1)

    sent(4, q_all, n_seq - 1)
    sent(5, acc_recv, n_seq - 1)
    sent(6, st_recv, n_seq - 1)
    sent(7, o_recv, n_seq - 1)
    sent(8, mid_all, n_seq - 1)
    sent(9, d_recv, n_seq - 1)
    sent(10, wo, n_seq - 1)


def solution(mesh):
    n_tok, n_seq, n_kv = mesh.shape["tok"], mesh.shape["seq"], mesh.shape["kv"]
    n_own = n_tok * n_kv
    lanes = np.arange(128) % 32
    freq = (ROPE_BASE ** (-(lanes * 2.0 / 64))).astype(np.float32).reshape(1, 128)

    def per_device(
        token_ids,
        request_order,
        cache_lengths,
        embed_table,
        attn_gain,
        proj_query,
        proj_kv,
        kv_cache,
        proj_out,
        mlp_gain,
        proj_gate,
        proj_up,
        proj_down,
    ):
        n_req, steps = token_ids.shape
        ctx = kv_cache.shape[1]
        rows = n_req * steps
        r_own, r_seq = rows // n_own, rows // n_seq
        width = proj_query.shape[0]
        vmem = pl.BlockSpec(memory_space=pltpu.VMEM)
        hbm = pl.BlockSpec(memory_space=pl.ANY)
        weights = [
            embed_table,
            proj_query,
            proj_kv.reshape(width, 128),
            kv_cache.reshape(n_req, ctx, 128),
            proj_out,
            proj_gate,
            proj_up,
            proj_down,
        ]
        scratch = [
            pltpu.SMEM((steps, n_req), jnp.int32),
            pltpu.SMEM((n_req,), jnp.int32),
            pltpu.SMEM((n_req,), jnp.int32),
            pltpu.VMEM((n_seq, 128), BF16),
            pltpu.VMEM((n_seq, 128), BF16),
            pltpu.VMEM((1, 128), F32),
        ]
        held = [w.shape for w in weights]
        held[4] = (n_seq, *proj_out.shape)
        scratch += [pltpu.VMEM(shape, BF16) for shape in held]
        scratch += [
            pltpu.VMEM((n_req // 2, ctx, 128), BF16),
            pltpu.VMEM((n_seq, 128), F32),
            pltpu.VMEM((rows, 128), jnp.int32),
            pltpu.VMEM((n_own, r_own, 128), BF16),
            pltpu.VMEM((n_own, r_own, 128), BF16),
            pltpu.VMEM((n_seq // n_own, r_seq, 128), BF16),
            pltpu.VMEM((n_seq, r_seq, 128), BF16),
            pltpu.VMEM((n_seq, 2 * r_seq, 128), BF16),
            pltpu.VMEM((ctx, 128), F32),
            pltpu.VMEM((ctx, 128), F32),
            pltpu.VMEM((128, ctx), BF16),
            pltpu.VMEM((128, ctx), BF16),
            pltpu.VMEM((n_seq, 2 * r_seq, 128), BF16),
            pltpu.VMEM((n_seq, 2 * r_seq, 128), BF16),
            pltpu.VMEM((n_req // 8, 2, 128), F32),
            pltpu.VMEM((n_seq, 2, 128), F32),
            pltpu.VMEM((128, 128), F32),
            pltpu.VMEM((n_seq, r_seq, 128), BF16),
            pltpu.VMEM((n_seq, r_seq, 128), BF16),
            pltpu.VMEM((n_seq, r_own, 128), BF16),
            pltpu.VMEM((n_seq, r_own, 128), BF16),
            pltpu.VMEM((n_seq, r_own, 128), BF16),
            pltpu.SemaphoreType.DMA((21,)),
            pltpu.SemaphoreType.DMA((11,)),
            pltpu.SemaphoreType.DMA((1, n_own)),
            pltpu.SemaphoreType.DMA((8, n_seq)),
        ]
        return pl.pallas_call(
            functools.partial(layer_kernel, n_tok, n_seq, n_kv),
            out_shape=jax.ShapeDtypeStruct((n_req // n_own, steps, 128), BF16),
            in_specs=[hbm] * (6 + len(weights)),
            out_specs=vmem,
            scratch_shapes=scratch,
            compiler_params=pltpu.CompilerParams(
                collective_id=0, has_side_effects=True, vmem_limit_bytes=64 * 1000 * 1000
            ),
            name="layer",
        )(
            token_ids.T,
            request_order,
            cache_lengths,
            attn_gain.reshape(n_seq, 128),
            mlp_gain.reshape(n_seq, 128),
            jnp.asarray(freq),
            *weights,
        )

    placed = (
        P(),
        P(),
        P(),
        P(("tok", "kv"), "seq"),
        P(),
        P(None, ("tok", "kv")),
        P(None, ("tok", "kv"), None),
        P(None, "seq", ("tok", "kv"), None),
        P(("tok", "kv"), "seq"),
        P(),
        P(None, "seq"),
        P(None, "seq"),
        P("seq", None),
    )
    return jax.shard_map(
        per_device,
        mesh=mesh,
        in_specs=placed,
        out_specs=P(("tok", "kv"), None, "seq"),
        check_vma=False,
    )
```
